128 devices in a mesh: ens: 8 (over y_lo, z), rep: 16 (over y_hi, x, core).
Axes of the slice: x: 4, y: 4 (y_hi: 2, y_lo: 2; y = y_hi * 2 + y_lo), z: 4, core: 2. Of those that a mesh axis runs over, the one named last changes fastest.
Arguments:
- cur_states: bfloat16 [32768, 4096], P('rep'), may hold values from -6 to 6
- buffer: bfloat16 [4096, 4096], P('rep'), may hold values from -6 to 6
- fetch_rows: int32 [16, 16, 128], P('rep'), may hold values from 0 to 255
- fetch_counts: int32 [16, 16], replicated, may hold values from 1 to 128, as said below
- actions: int32 [32768], P('rep'), may hold values from 0 to 255
- rewards: float32 [32768], P('rep'), may hold values from -0.5 to 0.5
- terminal: int32 [32768], P('rep'), may hold values 0 or 1
- mc_return: float32 [32768], P('rep'), may hold values from 0 to 1
- w_in: bfloat16 [8, 4096, 512], P('ens'), may hold values from -0.09375 to 0.09375
- w_out: bfloat16 [8, 512, 256], P('ens'), may hold values from -0.25 to 0.25
Outputs:
- targets: float32 [32768], P('rep')
- grad_in: float32 [8, 4096, 512], P('ens', 'rep')
- grad_out: float32 [8, 512, 256], P('ens', 'rep')
The draws below stay inside these ranges and needn't reach their ends.
Inputs may be any that keep to these rules, and one draw needn't show every extreme that they name: `fetch_rows`: each entry indexes the owner's own rows. `fetch_counts`: entry [o, r] is how many leading slots of requester r at owner o are used; some entry equals 128 in every draw.
All inputs are finite; a program needn't handle non-finite values. No bound on the sum of `terminal` on one device may be relied on, other than what follows from the above.
Results may differ from the reference program's by a relative error of at most 0.0044.
Values may be sent and summed in bfloat16 or wider, within the bound.
No kernel may reach another device: no remote copies, remote signals or barrier semaphores. Data moves between devices by JAX's collectives and lax.ppermute only.
A program may use at most 192 MiB of HBM per device.

```python
import jax
import jax.numpy as jnp
from jax import lax

D = 4096
HEAD = 512
BINS = 256
CAP = 128
BUF_DEV = 256
MEMBERS = 8
OWNERS = 16
TRANS_ALL = 32768


def draw_fetch_counts(key, part):
    key_counts, key_owner = jax.random.split(jax.random.fold_in(key, 7))
    requester = jnp.arange(OWNERS, dtype=jnp.int32)
    upper = CAP // 3 + (CAP - CAP // 3) * requester // max(OWNERS - 1, 1)
    random_bits = jax.random.randint(key_counts, (OWNERS, OWNERS), 0, 1 << 20)
    counts = 1 + random_bits % upper[None, :]
    chosen_owner = jax.random.randint(key_owner, (), 0, OWNERS)
    owner_ids = jnp.arange(OWNERS, dtype=jnp.int32)[:, None]
    counts = jnp.where((owner_ids == chosen_owner) & (requester[None, :] == OWNERS - 1), CAP, counts)
    return counts.astype(jnp.int32)


def place_ends(drawn, rng, smallest, largest):
    shape = drawn.shape
    place = [jax.random.randint(jax.random.fold_in(rng, axis), (), 0, shape[axis]) for axis in range(len(shape))]
    drawn = drawn.at[tuple(place)].set(smallest)
    longest = shape.index(max(shape))
    place[longest] = (place[longest] + 1) % shape[longest]
    return drawn.at[tuple(place)].set(largest)


def levels(rng, dims, shards, smallest, largest):
    loudness, own = 1.0, jax.random.fold_in(rng, 6)
    for position, shards_of in shards:
        heights = jnp.exp(jax.random.uniform(jax.random.fold_in(own, position), (shards_of,), jnp.float32, smallest / len(shards), largest / len(shards)))
        loudness = loudness * jnp.repeat(heights, dims[position] // shards_of).reshape([-1 if axis == position else 1 for axis in range(len(dims))])
    return loudness


def gaussian(rng, shape, width, reach, pieces=(), held_as=jnp.bfloat16):
    array = width * jax.random.normal(rng, shape, jnp.float32)
    if pieces:
        array = array * levels(rng, shape, pieces, -0.22, 0.18)
    return jnp.clip(array, -reach, reach).astype(held_as)


def setup_inputs(seed: int = 0) -> dict:
    streams_of = jax.random.split(jax.random.key(seed), 11)
    cur_states = gaussian(streams_of[0], (TRANS_ALL, D), 1.0, 6.0, ((0, 16),))
    buffer = gaussian(streams_of[1], (BUF_DEV * OWNERS, D), 1.0, 6.0, ((0, 16),))
    fetch_rows = place_ends(jax.random.randint(streams_of[2], (OWNERS, OWNERS, CAP), 0, BUF_DEV), jax.random.fold_in(streams_of[2], 1), 0, BUF_DEV - 1).astype(jnp.int32)
    fetch_counts = draw_fetch_counts(jax.random.fold_in(streams_of[10], 71), 0)
    actions = place_ends(jax.random.randint(streams_of[4], (TRANS_ALL,), 0, BINS), jax.random.fold_in(streams_of[4], 1), 0, BINS - 1).astype(jnp.int32)
    rewards = jnp.clip(jax.random.uniform(streams_of[5], (TRANS_ALL,), jnp.float32, -0.5, 0.5) * levels(streams_of[5], (TRANS_ALL,), ((0, 16),), -0.4, 0.0), -0.5, 0.5)
    terminal = place_ends((jax.random.randint(streams_of[6], (TRANS_ALL,), 0, 4) < 1).astype(jnp.int32), jax.random.fold_in(streams_of[6], 1), 0, 1)
    mc_return = jnp.clip(1.0 * jax.random.uniform(streams_of[7], (TRANS_ALL,), jnp.float32) ** levels(streams_of[7], (TRANS_ALL,), ((0, 16),), -0.2, 0.2), 0.0, 1.0)
    w_in = gaussian(streams_of[8], (MEMBERS, D, HEAD), D ** -0.5, 0.09375, ((0, 8),))
    w_out = gaussian(streams_of[9], (MEMBERS, HEAD, BINS), HEAD ** -0.5, 0.25, ((0, 8),))
    return dict(cur_states=cur_states, buffer=buffer, fetch_rows=fetch_rows, fetch_counts=fetch_counts, actions=actions, rewards=rewards, terminal=terminal, mc_return=mc_return, w_in=w_in, w_out=w_out)


def critic_head(features, w_first, w_second):
    preact = jnp.dot(features, w_first, preferred_element_type=jnp.float32)
    sigmoid_pre = jax.nn.sigmoid(preact)
    hidden = (preact * sigmoid_pre).astype(jnp.bfloat16)
    values = jax.nn.sigmoid(jnp.dot(hidden, w_second, preferred_element_type=jnp.float32))
    return preact, sigmoid_pre, hidden, values


def reference(cur_states, buffer, fetch_rows, fetch_counts, actions, rewards, terminal, mc_return, w_in, w_out):
    owner_ids = jnp.arange(OWNERS, dtype=jnp.int32)
    positions = (owner_ids[:, None, None] * BUF_DEV + fetch_rows).astype(jnp.int32)
    positions = jnp.transpose(positions, (1, 0, 2)).reshape(-1)
    slot_ids = jnp.arange(CAP, dtype=jnp.int32)
    used = (slot_ids[None, None, :] < jnp.transpose(fetch_counts)[:, :, None]).reshape(-1).astype(jnp.float32)
    counted = jnp.sum(fetch_counts).astype(jnp.float32)
    upcoming = jnp.take(buffer, positions, axis=0)

    def next_best(weights):
        return jnp.max(critic_head(upcoming, weights[0], weights[1])[3], axis=1)

    best_next = lax.map(next_best, (w_in, w_out))
    ens_floor = jnp.min(best_next, axis=0)
    bootstrap = jnp.maximum(ens_floor, mc_return)
    target = rewards + 0.98 * (1.0 - terminal.astype(jnp.float32)) * bootstrap
    targets = used * target
    chosen = actions[:, None] == jnp.arange(BINS, dtype=jnp.int32)[None, :]

    def member_grads(weights):
        w_first, w_second = weights
        preact, sigmoid_pre, hidden, values = critic_head(cur_states, w_first, w_second)
        taken = jnp.sum(jnp.where(chosen, values, 0.0), axis=1)
        errors = used * 2.0 * (taken - target) * taken * (1.0 - taken) * (65536.0 / counted)
        d_logits = jnp.where(chosen, errors[:, None], 0.0).astype(jnp.bfloat16)
        grad_second = lax.dot_general(hidden, d_logits, (((0,), (0,)), ((), ())), preferred_element_type=jnp.float32)
        back = lax.dot_general(d_logits, w_second, (((1,), (1,)), ((), ())), preferred_element_type=jnp.float32)
        d_hidden = (back * sigmoid_pre * (1.0 + preact * (1.0 - sigmoid_pre))).astype(jnp.bfloat16)
        grad_first = lax.dot_general(cur_states, d_hidden, (((0,), (0,)), ((), ())), preferred_element_type=jnp.float32)
        return grad_first, grad_second

    grad_in, grad_out = lax.map(member_grads, (w_in, w_out))
    return targets, grad_in, grad_out
```

```python
import jax
import jax.numpy as jnp
from jax import lax
from jax.sharding import PartitionSpec as P


def place(y, x, core):
    return y * 8 + x * 2 + core


def moves(fn):
    return [
        (place(y, x, c), place(*fn(y, x, c)))
        for y in range(2)
        for x in range(4)
        for c in range(2)
    ]


CORE = moves(lambda y, x, c: (y, x, 1 - c))
RIGHT = moves(lambda y, x, c: (y, (x + 1) % 4, c))
LEFT = moves(lambda y, x, c: (y, (x + 3) % 4, c))
ACROSS = moves(lambda y, x, c: (1 - y, x, c))


def sent(value, pairs):
    return lax.ppermute(value, "rep", pairs)


def low(value):
    return value.astype(jnp.bfloat16)


def high(value):
    return value.astype(jnp.float32)


def reduced(piece, y, x, core):
    far, right, left = (x + 2) & 3, (x + 1) & 3, (x + 3) & 3
    other, same = 1 - y, y
    partner = 1 - core

    def pair(x_at):
        away = sent(jnp.stack([low(piece(h, x_at, partner)) for h in (other, same)]), CORE)
        kept = [piece(h, x_at, core) for h in (other, same)]
        return [k + high(away[i]) for i, k in enumerate(kept)]

    far_other, far_same = pair(far)
    from_left_far = sent(low(far_other), RIGHT)
    from_right_far = sent(low(far_same), LEFT)
    right_other, right_same = pair(right)
    left_other, left_same = pair(left)
    from_left_same = sent(low(right_same), RIGHT)
    from_right_other = sent(low(left_other), LEFT)
    from_left_other = sent(low(right_other + high(from_left_far)), RIGHT)
    from_right_same = sent(low(left_same + high(from_right_far)), LEFT)
    own_other, own_same = pair(x)
    own_other = own_other + high(from_right_other) + high(from_left_other)
    over = sent(low(own_other), ACROSS)
    own_same = own_same + high(from_left_same) + high(from_right_same)
    return own_same + high(over)


def sent_to_all(shard, axis):
    count = lax.axis_size(axis)
    return lax.all_to_all(
        jnp.broadcast_to(shard[None], (count, *shard.shape)), axis, 0, 0, tiled=True
    )


def critic_head(features, w_first, w_second):
    preact = jnp.dot(features, w_first, preferred_element_type=jnp.float32)
    sigmoid_pre = jax.nn.sigmoid(preact)
    hidden = (preact * sigmoid_pre).astype(jnp.bfloat16)
    logits = jnp.dot(hidden, w_second, preferred_element_type=jnp.float32)
    return (preact, sigmoid_pre, hidden, logits)


def shards(
    cur_states, buffer, fetch_rows, fetch_counts, actions, rewards, terminal, mc_return, w_in, w_out
):
    my_index = lax.axis_index("rep").astype(jnp.uint32)
    core, x, y = my_index & 1, (my_index >> 1) & 3, my_index >> 3
    slots_per = fetch_rows.shape[2]
    w_first = w_in[0]
    w_second = w_out[0]
    my_counts = lax.dynamic_slice_in_dim(fetch_counts, my_index, 1, 1)[:, 0]
    slot_ids = jnp.arange(slots_per, dtype=jnp.int32)
    used = (slot_ids[None, :] < my_counts[:, None]).reshape(-1).astype(jnp.float32)
    counted = jnp.sum(fetch_counts).astype(jnp.float32)

    row_best = jax.nn.sigmoid(jnp.max(critic_head(buffer, w_first, w_second)[3], axis=1))
    row_floor = sent_to_all(row_best, "ens").min(axis=0)
    row_ids = jnp.arange(buffer.shape[0], dtype=jnp.int32)
    served = jnp.sum(
        jnp.where(fetch_rows[0][:, :, None] == row_ids[None, None, :], row_floor, 0.0), axis=2
    )
    ens_floor = lax.all_to_all(served, "rep", split_axis=0, concat_axis=0, tiled=True).reshape(-1)

    bootstrap = jnp.maximum(ens_floor, mc_return)
    target = rewards + 0.98 * (1.0 - terminal.astype(jnp.float32)) * bootstrap
    targets = used * target
    chosen = actions[:, None] == jnp.arange(w_second.shape[1], dtype=jnp.int32)[None, :]
    preact, sigmoid_pre, hidden, logits = critic_head(cur_states, w_first, w_second)
    taken = jax.nn.sigmoid(jnp.sum(jnp.where(chosen, logits, 0.0), axis=1))
    errors = used * 2.0 * (taken - target) * taken * (1.0 - taken) * (65536.0 / counted)
    d_logits = jnp.where(chosen, errors[:, None], 0.0).astype(jnp.bfloat16)
    grad_second = lax.dot_general(
        hidden, d_logits, (((0,), (0,)), ((), ())), preferred_element_type=jnp.float32
    )
    back = lax.dot_general(
        d_logits, w_second, (((1,), (1,)), ((), ())), preferred_element_type=jnp.float32
    )
    d_hidden = (back * sigmoid_pre * (1.0 + preact * (1.0 - sigmoid_pre))).astype(jnp.bfloat16)
    d_hidden = lax.optimization_barrier(d_hidden)

    depth = cur_states.shape[1] // 16
    rows_second = grad_second.shape[0] // 16

    def piece(y_at, x_at, core_at):
        at = place(y_at, x_at, core_at)
        columns = lax.dynamic_slice_in_dim(cur_states, at * depth, depth, 1)
        first = lax.dot_general(
            d_hidden, columns, (((0,), (0,)), ((), ())), preferred_element_type=jnp.float32
        )
        second = lax.dynamic_slice_in_dim(grad_second, at * rows_second, rows_second, 0)
        return jnp.concatenate([first, second])

    share = reduced(piece, y, x, core)
    width = w_first.shape[1]
    return (targets, share[:width].T[None], share[width:][None])


def solution(mesh):
    placed = (
        P("rep", None),
        P("rep", None),
        P("rep", None, None),
        P(),
        P("rep"),
        P("rep"),
        P("rep"),
        P("rep"),
        P("ens", None, None),
        P("ens", None, None),
    )
    return jax.shard_map(
        shards,
        mesh=mesh,
        in_specs=placed,
        out_specs=(P("rep"), P("ens", "rep", None), P("ens", "rep", None)),
        check_vma=False,
    )
```

```python
import functools

import jax
import jax.numpy as jnp
from jax import lax
from jax.experimental import pallas as pl
from jax.experimental.pallas import tpu as pltpu
from jax.sharding import PartitionSpec as P

UNIT = 16
BLOCK = 256
F32, BF16 = jnp.float32, jnp.bfloat16
VMEM = pl.BlockSpec(memory_space=pltpu.VMEM)
SMEM = pl.BlockSpec(memory_space=pltpu.SMEM)
HBM = pl.BlockSpec(memory_space=pltpu.HBM)


def place(y, x, core):
    return y * 8 + x * 2 + core


def moves(fn):
    return [
        (place(y, x, c), place(*fn(y, x, c)))
        for y in range(2)
        for x in range(4)
        for c in range(2)
    ]


CORE = moves(lambda y, x, c: (y, x, 1 - c))
RIGHT = moves(lambda y, x, c: (y, (x + 1) % 4, c))
LEFT = moves(lambda y, x, c: (y, (x + 3) % 4, c))
ACROSS = moves(lambda y, x, c: (1 - y, x, c))


def sent(value, pairs):
    return lax.ppermute(value, "rep", pairs)


def low(value):
    return value.astype(BF16)


def high(value):
    return value.astype(F32)


def after(value, *others):
    return lax.optimization_barrier((value, *others))


def call(
    kernel, name, out_shape, in_specs, scratch=(), out_specs=None, limit=16, flops=0,
    bytes_moved=1 << 20,
):
    single = not isinstance(out_shape, (list, tuple))
    if out_specs is None:
        out_specs = VMEM if single else [VMEM] * len(out_shape)
    return pl.pallas_call(
        kernel,
        name=name,
        out_shape=out_shape,
        in_specs=in_specs,
        out_specs=out_specs,
        scratch_shapes=list(scratch),
        compiler_params=pltpu.CompilerParams(vmem_limit_bytes=limit << 20),
        cost_estimate=pl.CostEstimate(
            flops=flops, bytes_accessed=bytes_moved, transcendentals=0
        ),
    )


def in_hbm(array):
    return pltpu.with_memory_space_constraint(array, pltpu.HBM)


def shape(dims, dtype=F32):
    return jax.ShapeDtypeStruct(dims, dtype)


def units_of(count):
    return (count + (UNIT - 1)) >> 4


def gathered(counts_ref, states_ref, packed_ref, sem_at):
    me = lax.axis_index("rep")
    owners = counts_ref.shape[0]
    runs = states_ref.shape[0] // owners // UNIT

    def start(source, position):
        pltpu.make_async_copy(
            states_ref.at[pl.ds(pl.multiple_of(source * UNIT, UNIT), UNIT)],
            packed_ref.at[pl.ds(pl.multiple_of(position * UNIT, UNIT), UNIT)],
            sem_at(position >> 4),
        ).start()

    def owner(o, position):
        def unit(u, position):
            start(o * runs + u, position)
            return position + 1

        return lax.fori_loop(0, units_of(counts_ref[o, me]), unit, position)

    units = lax.fori_loop(0, owners, owner, jnp.int32(0))
    blocks = (units + (BLOCK // UNIT - 1)) >> 4
    lax.fori_loop(units, blocks * (BLOCK // UNIT), lambda p, c: (start(0, p), c)[1], 0)
    return blocks


def gathered_block(states_ref, packed_ref, sem):
    return pltpu.make_async_copy(states_ref.at[pl.ds(0, BLOCK)], packed_ref.at[pl.ds(0, BLOCK)], sem)


def pack_rows(counts_ref, values, packed_refs):
    me = lax.axis_index("rep")
    owners, cap = values[0].shape
    lane = lax.broadcasted_iota(jnp.int32, (1, cap), 1)
    for ref in packed_refs:
        ref[...] = jnp.zeros_like(ref)
    start = jnp.int32(0)
    for o in range(owners):
        count = counts_ref[o, me]
        row, shift = start >> 7, start & 127
        for value, ref in zip(values, packed_refs):
            kept = jnp.where(lane < count, value[o : o + 1, :], 0.0)
            turned = pltpu.roll(kept, shift, 1)
            ref[pl.ds(row, 1), :] += jnp.where(lane >= shift, turned, 0.0)
            ref[pl.ds(row + 1, 1), :] += jnp.where(lane < shift, turned, 0.0)
        start = start + units_of(count) * UNIT


def next_kernel(
    buffer_ref, w_in_ref, w_out_ref, fetch_ref, picked_ref, w_ref, rows_ref, w_second, fetch, total,
    sems, small_sems,
):
    steps = sems.shape[1]
    depth = w_in_ref.shape[0] // steps
    copies = []
    for i in range(steps):
        part = pl.ds(i * depth, depth)
        pair = (
            pltpu.make_async_copy(w_in_ref.at[part], w_ref.at[part], sems.at[0, i]),
            pltpu.make_async_copy(buffer_ref.at[:, part], rows_ref.at[:, part], sems.at[1, i]),
        )
        for copy in pair:
            copy.start()
        copies.append(pair)
    second = pltpu.make_async_copy(w_out_ref, w_second, small_sems.at[0])
    wanted = pltpu.make_async_copy(fetch_ref, fetch, small_sems.at[1])
    second.start()
    wanted.start()
    for i in range(steps):
        for copy in copies[i]:
            copy.wait()
        part = pl.ds(i * depth, depth)
        term = jnp.dot(rows_ref[:, part], w_ref[part, :], preferred_element_type=F32)
        total[...] = term if i == 0 else total[...] + term
    preact = total[...]
    hidden = low(preact * jax.nn.sigmoid(preact))
    second.wait()
    wanted.wait()
    logits = jnp.dot(hidden, w_second[...], preferred_element_type=F32)
    best = jax.nn.sigmoid(jnp.max(logits, axis=1, keepdims=True))
    halves = [jnp.broadcast_to(best[i : i + 128], (128, 128)).T[:8] for i in (0, 128)]
    for i in range(0, fetch.shape[0], 8):
        rows = fetch[pl.ds(i, 8), :]
        found = [
            jnp.take_along_axis(half, rows & 127, axis=1, mode="promise_in_bounds")
            for half in halves
        ]
        picked = jnp.where(rows < 128, found[0], found[1])
        for d in range(picked_ref.shape[0]):
            picked_ref[d, pl.ds(i, 8), :] = picked


def forward_kernel(
    counts_ref, states_ref, w_in_ref, w_out_ref, actions_ref,
    slope_ref, hidden_ref, small_ref,
    packed, w_first, w_second, actions, small, slope, hidden, sems, load_sems, out_sems,
):
    owners = actions_ref.shape[0]
    loads = [
        pltpu.make_async_copy(source, target, load_sems.at[i])
        for i, (source, target) in enumerate(
            ((w_in_ref, w_first), (w_out_ref, w_second), (actions_ref, actions))
        )
    ]
    for load in loads:
        load.start()
    blocks = gathered(counts_ref, states_ref, packed, lambda b: sems.at[b])
    loads[2].wait()
    taken_ref, act_ref = small.at[pl.ds(0, owners)], small.at[pl.ds(owners, owners + 8)]
    pack_rows(counts_ref, [high(actions[...])], [act_ref])
    taken_ref[...] = jnp.zeros_like(taken_ref)
    loads[1].wait()
    w_out = w_second[...]
    w_out_turned = w_out.T
    bins = lax.broadcasted_iota(jnp.int32, (w_out.shape[1], BLOCK), 0).astype(F32)
    loads[0].wait()

    def kept(b, slot):
        return (
            pltpu.make_async_copy(slope.at[slot], slope_ref.at[b], out_sems.at[slot]),
            pltpu.make_async_copy(hidden.at[slot], hidden_ref.at[b], out_sems.at[2 + slot]),
        )

    def step(b, carry):
        slot = b & 1
        gathered_block(states_ref, packed, sems.at[b]).wait()
        part = pl.ds(pl.multiple_of(b * BLOCK, BLOCK), BLOCK)
        preact = jnp.dot(packed[part, :], w_first[...], preferred_element_type=F32).T

        @pl.when(b >= 2)
        def _():
            for copy in kept(b - 2, slot):
                copy.wait()

        sigmoid_pre = jax.nn.sigmoid(preact)
        hid = low(preact * sigmoid_pre)
        hidden[slot] = hid
        logits = jnp.dot(w_out_turned, hid, preferred_element_type=F32)
        acts = jnp.concatenate([act_ref[pl.ds(2 * b + i, 1), :] for i in (0, 1)], axis=1)
        chosen = bins == acts
        taken = jax.nn.sigmoid(jnp.sum(jnp.where(chosen, logits, 0.0), axis=0, keepdims=True))
        for i in (0, 1):
            taken_ref[pl.ds(2 * b + i, 1), :] = taken[:, i * 128 : (i + 1) * 128]
        row = jnp.dot(w_out, chosen.astype(F32).astype(BF16), preferred_element_type=F32)
        slope[slot] = row * (sigmoid_pre * (1.0 + preact * (1.0 - sigmoid_pre)))
        for copy in kept(b, slot):
            copy.start()
        return carry

    lax.fori_loop(0, blocks, step, 0)
    last = pltpu.make_async_copy(small, small_ref, load_sems.at[2])
    last.start()

    @pl.when(blocks >= 2)
    def _():
        for copy in kept(blocks - 2, blocks & 1):
            copy.wait()

    for copy in kept(blocks - 1, (blocks - 1) & 1):
        copy.wait()
    last.wait()


def error_kernel(
    counts_ref, states_ref, slope_ref, hidden_ref, small_ref,
    table_ref, best_ref, rewards_ref, terminal_ref, returns_ref,
    targets_ref, packed_ref, d_hidden_ref, grad_ref, blocks_ref,
    slope, hidden, small, table, rewards, terminal, returns, target_row, scale_row,
    sems, block_sems, packed_sems,
):
    me = lax.axis_index("rep")
    owners, cap = rewards.shape
    loads = [
        pltpu.make_async_copy(source, target, sems.at[i])
        for i, (source, target) in enumerate(
            (
                (small_ref, small), (table_ref, table), (rewards_ref, rewards),
                (terminal_ref, terminal), (returns_ref, returns),
            )
        )
    ]
    for load in loads:
        load.start()
    units = lax.fori_loop(
        0, owners, lambda o, n: n + units_of(counts_ref[o, me]), jnp.int32(0)
    )
    blocks = (units + (BLOCK // UNIT - 1)) >> 4

    def block(b):
        return (
            pltpu.make_async_copy(slope_ref.at[b], slope.at[b], block_sems.at[0, b]),
            pltpu.make_async_copy(hidden_ref.at[b], hidden.at[b], block_sems.at[1, b]),
        )

    def load_block(b, carry):
        for copy in block(b):
            copy.start()
        return carry

    lax.fori_loop(0, blocks, load_block, 0)
    gathered(counts_ref, states_ref, packed_ref, lambda b: packed_sems.at[b])
    blocks_ref[...] = jnp.full(blocks_ref.shape, blocks, jnp.int32)
    for load in loads:
        load.wait()
    counts = table[...]
    counted = jnp.sum(counts).astype(F32)
    requester = lax.broadcasted_iota(jnp.int32, counts.shape, 1)
    mine = jnp.sum(jnp.where(requester == me, counts, 0), axis=1, keepdims=True)
    used = (lax.broadcasted_iota(jnp.int32, (owners, cap), 1) < mine).astype(F32)
    bootstrap = jnp.maximum(jnp.min(best_ref[...], axis=0), returns[...])
    target = rewards[...] + 0.98 * (1.0 - terminal[...].astype(F32)) * bootstrap
    targets_ref[...] = used * target
    scale = used * 2.0 * (jnp.full((owners, cap), 65536.0, F32) / counted)
    pack_rows(counts_ref, [target, scale], [target_row, scale_row])
    taken = small[pl.ds(0, owners), :]
    errors = (taken - target_row[pl.ds(0, owners), :]) * taken * (1.0 - taken)
    scale_row[pl.ds(0, owners), :] = high(low(errors * scale_row[pl.ds(0, owners), :]))
    grad_ref[...] = jnp.zeros_like(grad_ref)
    bins = lax.broadcasted_iota(jnp.int32, (grad_ref.shape[1], BLOCK), 0).astype(F32)

    def step(b, carry):
        at = pl.ds(pl.multiple_of(b * BLOCK, BLOCK), BLOCK)
        errors, acts = [
            jnp.concatenate([ref[pl.ds(first + 2 * b + i, 1), :] for i in (0, 1)], axis=1)
            for ref, first in ((scale_row, 0), (small, owners))
        ]
        for copy in block(b):
            copy.wait()
        d_hidden_ref[:, at] = low(slope[b] * errors)
        d_logits = low(jnp.where(bins == acts, errors, 0.0))
        grad_ref[...] += lax.dot_general(
            hidden[b], d_logits, (((1,), (1,)), ((), ())), preferred_element_type=F32
        )
        return carry

    lax.fori_loop(0, blocks, step, 0)
    lax.fori_loop(
        0,
        blocks,
        lambda b, c: (gathered_block(states_ref, packed_ref, packed_sems.at[b]).wait(), c)[1],
        0,
    )


def piece_kernel(steps, with_recv, stacked, blocks_ref, d_hidden_ref, states_ref, grad_ref, *rest):
    recv_ref = rest[0] if with_recv else None
    out_refs, total = rest[with_recv:-1], rest[-1]
    me = lax.axis_index("rep")
    y, x, core = me >> 3, (me >> 1) & 3, me & 1
    blocks = blocks_ref[0, 0]
    _, width, depth = total.shape
    rows = grad_ref.shape[0] // 16
    ats = [place(y ^ dy, (x + dx) & 3, core ^ dc) for dy, dx, dc in steps]

    for count in range(1, d_hidden_ref.shape[1] // BLOCK + 1):

        @pl.when(blocks == count)
        def _(deep=count * BLOCK):
            def piece(j, carry):
                at = ats[-1]
                for k in range(len(ats) - 1):
                    at = jnp.where(j == k, ats[k], at)
                columns = pl.ds(pl.multiple_of(at * depth, depth), depth)
                total[j] = jnp.dot(
                    d_hidden_ref[:, :deep], states_ref[:deep, columns], preferred_element_type=F32
                )
                return carry

            lax.fori_loop(0, len(ats), piece, 0)

    for j, at in enumerate(ats):
        first = total[j]
        second = grad_ref[pl.ds(pl.multiple_of(at * rows, rows), rows), :]
        if with_recv:
            first = first + high(recv_ref[j, pl.ds(0, width), :])
            second = second + high(recv_ref[j, pl.ds(width, rows), :])
        out = out_refs[0].at[j] if stacked else out_refs[j]
        out[pl.ds(0, width), :] = first.astype(out.dtype)
        out[pl.ds(width, rows), :] = second.astype(out.dtype)


def final_kernel(own_ref, left_ref, right_ref, over_ref, first_ref, second_ref):
    width = first_ref.shape[1]
    total = own_ref[...] + high(left_ref[...]) + high(right_ref[...]) + high(over_ref[...])
    first_ref[...] = total[:width].T
    second_ref[...] = total[width:]


def shards(
    cur_states, buffer, fetch_rows, fetch_counts, actions, rewards, terminal, mc_return, w_in, w_out
):
    w_first, w_second = w_in[0], w_out[0]
    owners, cap = fetch_rows.shape[1:]
    slots, model = cur_states.shape
    width, bins = w_second.shape
    members = lax.axis_size("ens")
    grid = lambda a: a.reshape(owners, cap)

    picked = call(
        next_kernel,
        "next_values",
        shape((members, owners, cap)),
        [HBM] * 4,
        [
            pltpu.VMEM(w_first.shape, BF16),
            pltpu.VMEM(buffer.shape, BF16),
            pltpu.VMEM(w_second.shape, BF16),
            pltpu.VMEM((owners, cap), jnp.int32),
            pltpu.VMEM((buffer.shape[0], width), F32),
            pltpu.SemaphoreType.DMA((2, 8)),
            pltpu.SemaphoreType.DMA((2,)),
        ],
        limit=63,
        flops=2 * buffer.shape[0] * model * width,
        bytes_moved=6 << 20,
    )(buffer, w_first, w_second, fetch_rows[0])
    best = lax.all_to_all(
        picked.reshape(members * owners, 1, cap), ("ens", "rep"), 0, 0, tiled=True
    ).reshape(members, owners, cap)

    count = slots // BLOCK
    slope, hidden, small = call(
        forward_kernel,
        "forward",
        [
            pltpu.HBM((count, width, BLOCK), F32),
            pltpu.HBM((count, width, BLOCK), BF16),
            pltpu.HBM((2 * owners + 8, cap), F32),
        ],
        [SMEM, HBM, HBM, HBM, HBM],
        [
            pltpu.VMEM((slots, model), BF16),
            pltpu.VMEM(w_first.shape, BF16),
            pltpu.VMEM(w_second.shape, BF16),
            pltpu.VMEM((owners, cap), jnp.int32),
            pltpu.VMEM((2 * owners + 8, cap), F32),
            pltpu.VMEM((2, width, BLOCK), F32),
            pltpu.VMEM((2, width, BLOCK), BF16),
            pltpu.SemaphoreType.DMA((count,)),
            pltpu.SemaphoreType.DMA((3,)),
            pltpu.SemaphoreType.DMA((4,)),
        ],
        out_specs=[HBM] * 3,
        limit=63,
        flops=slots * model * width,
        bytes_moved=12 << 20,
    )(fetch_counts, cur_states, w_first, w_second, grid(actions))

    targets, packed, d_hidden, grad_second, blocks = call(
        error_kernel,
        "errors",
        [
            shape((owners, cap)),
            pltpu.VMEM((slots, model), BF16),
            pltpu.VMEM((width, slots), BF16),
            pltpu.VMEM((width, bins), F32),
            pltpu.VMEM((8, 128), jnp.int32),
        ],
        [SMEM] + [HBM] * 5 + [VMEM] + [HBM] * 3,
        [
            pltpu.VMEM((count, width, BLOCK), F32),
            pltpu.VMEM((count, width, BLOCK), BF16),
            pltpu.VMEM((2 * owners + 8, cap), F32),
            pltpu.VMEM(fetch_counts.shape, jnp.int32),
            pltpu.VMEM((owners, cap), F32),
            pltpu.VMEM((owners, cap), jnp.int32),
            pltpu.VMEM((owners, cap), F32),
            pltpu.VMEM((owners + 8, cap), F32),
            pltpu.VMEM((owners + 8, cap), F32),
            pltpu.SemaphoreType.DMA((5,)),
            pltpu.SemaphoreType.DMA((2, count)),
            pltpu.SemaphoreType.DMA((count,)),
        ],
        limit=45,
        flops=1 << 28,
        bytes_moved=14 << 20,
    )(
        fetch_counts, cur_states, *[in_hbm(a) for a in (slope, hidden, small, fetch_counts)],
        best, *[in_hbm(grid(a)) for a in (rewards, terminal, mc_return)],
    )

    depth = model // 16
    tall = width + width // 16

    def pieces(name, source, steps, dtypes=None, recv=None):
        stacked = dtypes is None
        out = (
            shape((len(steps), tall, depth), BF16)
            if stacked
            else [shape((tall, depth), t) for t in dtypes]
        )
        extra = () if recv is None else (recv,)
        return call(
            functools.partial(piece_kernel, steps, len(extra), stacked),
            name,
            out,
            [VMEM] * (4 + len(extra)),
            [pltpu.VMEM((len(steps), width, depth), F32)],
            flops=len(steps) * slots * width * depth,
            bytes_moved=len(steps) << 18,
        )(blocks, source, packed, grad_second, *extra)

    far = [(1, 2), (0, 2)]
    near = [(1, 1), (1, 3), (0, 1), (0, 3)]
    own = [(1, 0), (0, 0)]
    theirs = lambda group: tuple((*g, 1) for g in group)
    ours = lambda group: tuple((*g, 0) for g in group)

    source = d_hidden
    away_far = pieces("far_theirs", source, theirs(far))
    source, away_far = after(source, away_far)
    away_far = sent(away_far, CORE)
    away_near = pieces("near_theirs", source, theirs(near))
    source, away_near = after(source, away_near)
    away_near = sent(away_near, CORE)
    far_other, far_same = pieces("far_ours", source, ours(far), (BF16, BF16), away_far)
    source, far_other, far_same = after(source, far_other, far_same)
    from_left_far = sent(far_other, RIGHT)
    from_right_far = sent(far_same, LEFT)
    away_own = pieces("own_theirs", source, theirs(own))
    source, away_own = after(source, away_own)
    away_own = sent(away_own, CORE)
    right_other, left_other, right_same, left_same = pieces(
        "near_ours", source, ours(near), (F32, BF16, BF16, F32), away_near
    )
    source, right_other, left_other, right_same, left_same = after(
        source, right_other, left_other, right_same, left_same
    )
    from_right_other = sent(left_other, LEFT)
    relay_other = low(right_other + high(from_left_far))
    relay_other, right_same = after(relay_other, right_same)
    from_left_other = sent(relay_other, RIGHT)
    from_left_same = sent(right_same, RIGHT)
    own_other, own_same = pieces("own_ours", source, ours(own), (F32, F32), away_own)
    from_right_same = sent(low(left_same + high(from_right_far)), LEFT)
    own_other = own_other + high(from_right_other) + high(from_left_other)
    over = sent(low(own_other), ACROSS)
    first, second = call(
        final_kernel,
        "final",
        [shape((depth, width)), shape((width // 16, bins))],
        [VMEM] * 4,
    )(own_same, from_left_same, from_right_same, over)
    return (targets.reshape(-1), first[None], second[None])


def solution(mesh):
    placed = (
        P("rep", None),
        P("rep", None),
        P("rep", None, None),
        P(),
        P("rep"),
        P("rep"),
        P("rep"),
        P("rep"),
        P("ens", None, None),
        P("ens", None, None),
    )
    return jax.shard_map(
        shards,
        mesh=mesh,
        in_specs=placed,
        out_specs=(P("rep"), P("ens", "rep", None), P("ens", "rep", None)),
        check_vma=False,
    )
```

```python
import functools

import jax
import jax.numpy as jnp
from jax import lax
from jax.experimental import pallas as pl
from jax.experimental.pallas import tpu as pltpu
from jax.sharding import PartitionSpec as P


UNIT = 16
BLOCK = 256
F32, BF16 = jnp.float32, jnp.bfloat16
VMEM = pl.BlockSpec(memory_space=pltpu.VMEM)
SMEM = pl.BlockSpec(memory_space=pltpu.SMEM)
HBM = pl.BlockSpec(memory_space=pltpu.HBM)


def place(y, x, core):
    return y * 8 + x * 2 + core


def moves(fn):
    return [
        (place(y, x, c), place(*fn(y, x, c)))
        for y in range(2)
        for x in range(4)
        for c in range(2)
    ]


CORE = moves(lambda y, x, c: (y, x, 1 - c))
RIGHT = moves(lambda y, x, c: (y, (x + 1) % 4, c))
LEFT = moves(lambda y, x, c: (y, (x + 3) % 4, c))
ACROSS = moves(lambda y, x, c: (1 - y, x, c))


def sent(value, pairs):
    return lax.ppermute(value, "rep", pairs)


def low(value):
    return value.astype(BF16)


def high(value):
    return value.astype(F32)


def after(value, *others):
    return lax.optimization_barrier((value, *others))


def call(
    kernel, out_shape, in_specs, scratch=(), out_specs=None, limit=16, flops=0,
    bytes_moved=1 << 20,
):
    single = not isinstance(out_shape, (list, tuple))
    if out_specs is None:
        out_specs = VMEM if single else [VMEM] * len(out_shape)
    return pl.pallas_call(
        kernel,
        out_shape=out_shape,
        in_specs=in_specs,
        out_specs=out_specs,
        scratch_shapes=list(scratch),
        compiler_params=pltpu.CompilerParams(vmem_limit_bytes=limit << 20),
        cost_estimate=pl.CostEstimate(
            flops=flops, bytes_accessed=bytes_moved, transcendentals=0
        ),
    )


def in_hbm(array):
    return pltpu.with_memory_space_constraint(array, pltpu.HBM)


def shape(dims, dtype=F32):
    return jax.ShapeDtypeStruct(dims, dtype)


def units_of(count):
    return (count + (UNIT - 1)) >> 4


def gathered(counts_ref, states_ref, packed_ref, sem_at):
    me = lax.axis_index("rep")
    owners = counts_ref.shape[0]
    runs = states_ref.shape[0] // owners // UNIT

    def start(source, position):
        pltpu.make_async_copy(
            states_ref.at[pl.ds(pl.multiple_of(source * UNIT, UNIT), UNIT)],
            packed_ref.at[pl.ds(pl.multiple_of(position * UNIT, UNIT), UNIT)],
            sem_at(position >> 4),
        ).start()

    def owner(o, position):
        def unit(u, position):
            start(o * runs + u, position)
            return position + 1

        return lax.fori_loop(0, units_of(counts_ref[o, me]), unit, position)

    units = lax.fori_loop(0, owners, owner, jnp.int32(0))
    blocks = (units + (BLOCK // UNIT - 1)) >> 4
    lax.fori_loop(units, blocks * (BLOCK // UNIT), lambda p, c: (start(0, p), c)[1], 0)
    return blocks


def gathered_block(states_ref, packed_ref, sem):
    return pltpu.make_async_copy(states_ref.at[pl.ds(0, BLOCK)], packed_ref.at[pl.ds(0, BLOCK)], sem)


def pack_rows(counts_ref, values, packed_refs):
    me = lax.axis_index("rep")
    owners, cap = values[0].shape
    lane = lax.broadcasted_iota(jnp.int32, (1, cap), 1)
    for ref in packed_refs:
        ref[...] = jnp.zeros_like(ref)
    start = jnp.int32(0)
    for o in range(owners):
        count = counts_ref[o, me]
        row, shift = start >> 7, start & 127
        for value, ref in zip(values, packed_refs):
            kept = jnp.where(lane < count, value[o : o + 1, :], 0.0)
            turned = pltpu.roll(kept, shift, 1)
            ref[pl.ds(row, 1), :] += jnp.where(lane >= shift, turned, 0.0)
            ref[pl.ds(row + 1, 1), :] += jnp.where(lane < shift, turned, 0.0)
        start = start + units_of(count) * UNIT


def next_kernel(
    buffer_ref, w_in_ref, w_out_ref, fetch_ref, picked_ref, w_ref, rows_ref, w_second, fetch, total,
    found_rows, sems, small_sems,
):
    steps = sems.shape[1]
    depth = w_in_ref.shape[0] // steps
    copies = []
    for i in range(steps):
        part = pl.ds(i * depth, depth)
        pair = (
            pltpu.make_async_copy(w_in_ref.at[part], w_ref.at[part], sems.at[0, i]),
            pltpu.make_async_copy(buffer_ref.at[:, part], rows_ref.at[:, part], sems.at[1, i]),
        )
        for copy in pair:
            copy.start()
        copies.append(pair)
    second = pltpu.make_async_copy(w_out_ref, w_second, small_sems.at[0])
    wanted = pltpu.make_async_copy(fetch_ref, fetch, small_sems.at[1])
    second.start()
    wanted.start()
    for i in range(steps):
        for copy in copies[i]:
            copy.wait()
        part = pl.ds(i * depth, depth)
        term = jnp.dot(rows_ref[:, part], w_ref[part, :], preferred_element_type=F32)
        total[...] = term if i == 0 else total[...] + term
    preact = total[...]
    hidden = low(preact * jax.nn.sigmoid(preact))
    second.wait()
    wanted.wait()
    logits = jnp.dot(hidden, w_second[...], preferred_element_type=F32)
    best = jax.nn.sigmoid(jnp.max(logits, axis=1, keepdims=True))
    halves = [jnp.broadcast_to(best[i : i + 128], (128, 128)).T[:8] for i in (0, 128)]
    for i in range(0, fetch.shape[0], 8):
        rows = fetch[pl.ds(i, 8), :]
        found = [
            jnp.take_along_axis(half, rows & 127, axis=1, mode="promise_in_bounds")
            for half in halves
        ]
        picked = jnp.where(rows < 128, found[0], found[1])
        for d in range(found_rows.shape[0]):
            found_rows[d, pl.ds(i, 8), :] = picked
    out = pltpu.make_async_copy(found_rows, picked_ref, small_sems.at[2])
    out.start()
    out.wait()


def member_kernel(
    counts_ref, states_ref, w_first, w_second, table_ref, best_ref,
    actions_ref, rewards_ref, terminal_ref, returns_ref,
    targets_ref, packed_ref, d_hidden_ref, grad_ref, blocks_ref,
    preacts, target_row, scale_row, act_row, sems,
):
    me = lax.axis_index("rep")
    owners, cap = rewards_ref.shape
    blocks = gathered(counts_ref, states_ref, packed_ref, lambda b: sems.at[b])
    blocks_ref[...] = jnp.full(blocks_ref.shape, blocks, jnp.int32)
    counts = table_ref[...]
    counted = jnp.sum(counts).astype(F32)
    requester = lax.broadcasted_iota(jnp.int32, counts.shape, 1)
    mine = jnp.sum(jnp.where(requester == me, counts, 0), axis=1, keepdims=True)
    used = (lax.broadcasted_iota(jnp.int32, (owners, cap), 1) < mine).astype(F32)
    bootstrap = jnp.maximum(jnp.min(best_ref[...], axis=0), returns_ref[...])
    target = rewards_ref[...] + 0.98 * (1.0 - terminal_ref[...].astype(F32)) * bootstrap
    targets_ref[...] = used * target
    scale = used * 2.0 * (jnp.full((owners, cap), 65536.0, F32) / counted)
    pack_rows(
        counts_ref, [target, scale, high(actions_ref[...])], [target_row, scale_row, act_row]
    )
    grad_ref[...] = jnp.zeros_like(grad_ref)
    bins = lax.broadcasted_iota(jnp.int32, (grad_ref.shape[1], BLOCK), 0).astype(F32)
    w_out = w_second[...]
    w_out_turned = w_out.T

    def arrived(b):
        gathered_block(states_ref, packed_ref, sems.at[b]).wait()

    def begin(b):
        part = pl.ds(pl.multiple_of(b * BLOCK, BLOCK), BLOCK)
        preacts[b & 1] = jnp.dot(packed_ref[part, :], w_first[...], preferred_element_type=F32)

    def finish(b):
        at = pl.ds(pl.multiple_of(b * BLOCK, BLOCK), BLOCK)
        goal, scaled, acts = [
            jnp.concatenate([ref[pl.ds(2 * b + i, 1), :] for i in (0, 1)], axis=1)
            for ref in (target_row, scale_row, act_row)
        ]
        preact = preacts[b & 1].T
        sigmoid_pre = jax.nn.sigmoid(preact)
        hidden = low(preact * sigmoid_pre)
        logits = jnp.dot(w_out_turned, hidden, preferred_element_type=F32)
        chosen = bins == acts
        taken = jax.nn.sigmoid(jnp.sum(jnp.where(chosen, logits, 0.0), axis=0, keepdims=True))
        errors = (taken - goal) * taken * (1.0 - taken) * scaled
        d_logits = low(jnp.where(chosen, errors, 0.0))
        grad_ref[...] += lax.dot_general(
            hidden, d_logits, (((1,), (1,)), ((), ())), preferred_element_type=F32
        )
        back = jnp.dot(w_out, d_logits, preferred_element_type=F32)
        d_hidden_ref[:, at] = low(back * sigmoid_pre * (1.0 + preact * (1.0 - sigmoid_pre)))

    arrived(0)
    begin(jnp.int32(0))

    def step(b, carry):
        arrived(b)
        finish(b - 1)
        begin(b)
        return carry

    lax.fori_loop(1, blocks, step, 0)
    finish(blocks - 1)


def piece_kernel(steps, with_recv, stacked, blocks_ref, d_hidden_ref, states_ref, grad_ref, *rest):
    recv_ref = rest[0] if with_recv else None
    out_refs, total = rest[with_recv:-1], rest[-1]
    me = lax.axis_index("rep")
    y, x, core = me >> 3, (me >> 1) & 3, me & 1
    blocks = blocks_ref[0, 0]
    _, width, depth = total.shape
    rows = grad_ref.shape[0] // 16
    ats = [place(y ^ dy, (x + dx) & 3, core ^ dc) for dy, dx, dc in steps]

    for count in range(1, d_hidden_ref.shape[1] // BLOCK + 1):

        @pl.when(blocks == count)
        def _(deep=count * BLOCK):
            def piece(j, carry):
                at = ats[-1]
                for k in range(len(ats) - 1):
                    at = jnp.where(j == k, ats[k], at)
                columns = pl.ds(pl.multiple_of(at * depth, depth), depth)
                total[j] = jnp.dot(
                    d_hidden_ref[:, :deep], states_ref[:deep, columns], preferred_element_type=F32
                )
                return carry

            lax.fori_loop(0, len(ats), piece, 0)

    for j, at in enumerate(ats):
        first = total[j]
        second = grad_ref[pl.ds(pl.multiple_of(at * rows, rows), rows), :]
        if with_recv:
            first = first + high(recv_ref[j, pl.ds(0, width), :])
            second = second + high(recv_ref[j, pl.ds(width, rows), :])
        out = out_refs[0].at[j] if stacked else out_refs[j]
        out[pl.ds(0, width), :] = first.astype(out.dtype)
        out[pl.ds(width, rows), :] = second.astype(out.dtype)


def final_kernel(own_ref, left_ref, right_ref, over_ref, first_ref, second_ref):
    width = first_ref.shape[1]
    total = own_ref[...] + high(left_ref[...]) + high(right_ref[...]) + high(over_ref[...])
    first_ref[...] = total[:width].T
    second_ref[...] = total[width:]


def update(
    cur_states, buffer, fetch_rows, fetch_counts, actions, rewards, terminal, mc_return, w_in, w_out
):
    w_first, w_second = w_in[0], w_out[0]
    owners, cap = fetch_rows.shape[1:]
    slots, model = cur_states.shape
    width, bins = w_second.shape
    members = lax.axis_size("ens")
    grid = lambda a: a.reshape(owners, cap)

    picked, w_kept = call(
        next_kernel,
        [pltpu.HBM((members, owners, cap), F32), pltpu.VMEM(w_first.shape, BF16)],
        [HBM] * 4,
        [
            pltpu.VMEM(buffer.shape, BF16),
            pltpu.VMEM(w_second.shape, BF16),
            pltpu.VMEM((owners, cap), jnp.int32),
            pltpu.VMEM((buffer.shape[0], width), F32),
            pltpu.VMEM((members, owners, cap), F32),
            pltpu.SemaphoreType.DMA((2, 8)),
            pltpu.SemaphoreType.DMA((3,)),
        ],
        out_specs=[HBM, VMEM],
        flops=2 * buffer.shape[0] * model * width,
        bytes_moved=6 << 20,
    )(*[in_hbm(a) for a in (buffer, w_first, w_second, fetch_rows[0])])
    best = lax.all_to_all(
        picked.reshape(members * owners, 1, cap), ("ens", "rep"), 0, 0, tiled=True
    ).reshape(members, owners, cap)

    targets, packed, d_hidden, grad_second, blocks = call(
        member_kernel,
        [
            shape((owners, cap)),
            pltpu.VMEM((slots, model), BF16),
            pltpu.VMEM((width, slots), BF16),
            pltpu.VMEM((width, bins), F32),
            pltpu.VMEM((8, 128), jnp.int32),
        ],
        [SMEM, HBM] + [VMEM] * 8,
        [pltpu.VMEM((2, BLOCK, width), F32)]
        + [pltpu.VMEM((owners + 8, cap), F32)] * 3
        + [pltpu.SemaphoreType.DMA((slots // BLOCK,))],
        flops=slots * model * width,
        bytes_moved=14 << 20,
    )(
        fetch_counts, in_hbm(cur_states), w_kept, w_second, fetch_counts, best,
        grid(actions), grid(rewards), grid(terminal), grid(mc_return),
    )

    depth = model // 16
    tall = width + width // 16

    def pieces(source, steps, dtypes=None, recv=None):
        stacked = dtypes is None
        out = (
            shape((len(steps), tall, depth), BF16)
            if stacked
            else [shape((tall, depth), t) for t in dtypes]
        )
        extra = () if recv is None else (recv,)
        return call(
            functools.partial(piece_kernel, steps, len(extra), stacked),
            out,
            [VMEM] * (4 + len(extra)),
            [pltpu.VMEM((len(steps), width, depth), F32)],
            flops=len(steps) * slots * width * depth,
            bytes_moved=len(steps) << 18,
        )(blocks, source, packed, grad_second, *extra)

    far = [(1, 2), (0, 2)]
    near = [(1, 1), (1, 3), (0, 1), (0, 3)]
    own = [(1, 0), (0, 0)]
    theirs = lambda group: tuple((*g, 1) for g in group)
    ours = lambda group: tuple((*g, 0) for g in group)

    away_far = sent(pieces(d_hidden, theirs(far)), CORE)
    away_near = sent(pieces(d_hidden, theirs(near)), CORE)
    far_other, far_same = pieces(d_hidden, ours(far), (BF16, BF16), away_far)
    from_left_far = sent(far_other, RIGHT)
    from_right_far = sent(far_same, LEFT)
    away_own = sent(pieces(d_hidden, theirs(own)), CORE)
    right_other, left_other, right_same, left_same = pieces(
        d_hidden, ours(near), (F32, BF16, BF16, F32), away_near
    )
    from_right_other = sent(left_other, LEFT)
    own_other, own_same = pieces(d_hidden, ours(own), (F32, F32), away_own)
    right_other, left_same, own_same = after(right_other, left_same, own_same)
    from_left_other = sent(low(right_other + high(from_left_far)), RIGHT)
    from_right_same = sent(low(left_same + high(from_right_far)), LEFT)
    from_left_same = sent(right_same, RIGHT)
    own_other = own_other + high(from_right_other) + high(from_left_other)
    over = sent(low(own_other), ACROSS)
    first, second = call(
        final_kernel, [shape((depth, width)), shape((width // 16, bins))], [VMEM] * 4
    )(own_same, from_left_same, from_right_same, over)
    return (targets.reshape(-1), first[None], second[None])


def solution(mesh):
    placed = (
        P("rep", None),
        P("rep", None),
        P("rep", None, None),
        P(),
        P("rep"),
        P("rep"),
        P("rep"),
        P("rep"),
        P("ens", None, None),
        P("ens", None, None),
    )
    return jax.shard_map(
        update,
        mesh=mesh,
        in_specs=placed,
        out_specs=(P("rep"), P("ens", "rep", None), P("ens", "rep", None)),
        check_vma=False,
    )
```

```python
import functools

import jax
import jax.numpy as jnp
from jax import lax
from jax.experimental import pallas as pl
from jax.experimental.pallas import tpu as pltpu
from jax.sharding import PartitionSpec as P


UNIT = 16
BLOCK = 256
F32, BF16 = jnp.float32, jnp.bfloat16
VMEM = pl.BlockSpec(memory_space=pltpu.VMEM)
SMEM = pl.BlockSpec(memory_space=pltpu.SMEM)
HBM = pl.BlockSpec(memory_space=pltpu.HBM)


def place(y, x, core):
    return y * 8 + x * 2 + core


def moves(fn):
    return [
        (place(y, x, c), place(*fn(y, x, c)))
        for y in range(2)
        for x in range(4)
        for c in range(2)
    ]


CORE = moves(lambda y, x, c: (y, x, 1 - c))
RIGHT = moves(lambda y, x, c: (y, (x + 1) % 4, c))
LEFT = moves(lambda y, x, c: (y, (x + 3) % 4, c))
FAR = moves(lambda y, x, c: (y, (x + 2) % 4, c))
ACROSS = moves(lambda y, x, c: (1 - y, x, c))


def sent(value, pairs):
    return lax.ppermute(value, "rep", pairs)


def low(value):
    return value.astype(BF16)


def high(value):
    return value.astype(F32)


def after(value, *others):
    return lax.optimization_barrier((value, *others))


def call(
    kernel, out_shape, in_specs, scratch=(), out_specs=None, limit=16, flops=0,
    bytes_moved=1 << 20,
):
    single = not isinstance(out_shape, (list, tuple))
    if out_specs is None:
        out_specs = VMEM if single else [VMEM] * len(out_shape)
    return pl.pallas_call(
        kernel,
        out_shape=out_shape,
        in_specs=in_specs,
        out_specs=out_specs,
        scratch_shapes=list(scratch),
        compiler_params=pltpu.CompilerParams(vmem_limit_bytes=limit << 20),
        cost_estimate=pl.CostEstimate(
            flops=flops, bytes_accessed=bytes_moved, transcendentals=0
        ),
    )


def in_hbm(array):
    return pltpu.with_memory_space_constraint(array, pltpu.HBM)


def shape(dims, dtype=F32):
    return jax.ShapeDtypeStruct(dims, dtype)


def units_of(count):
    return (count + (UNIT - 1)) >> 4


def gathered(counts_ref, states_ref, packed_ref, sem_at):
    me = lax.axis_index("rep")
    owners = counts_ref.shape[0]
    runs = states_ref.shape[0] // owners // UNIT

    def start(source, position):
        pltpu.make_async_copy(
            states_ref.at[pl.ds(pl.multiple_of(source * UNIT, UNIT), UNIT)],
            packed_ref.at[pl.ds(pl.multiple_of(position * UNIT, UNIT), UNIT)],
            sem_at(position >> 4),
        ).start()

    def owner(o, position):
        def unit(u, position):
            start(o * runs + u, position)
            return position + 1

        return lax.fori_loop(0, units_of(counts_ref[o, me]), unit, position)

    units = lax.fori_loop(0, owners, owner, jnp.int32(0))
    blocks = (units + (BLOCK // UNIT - 1)) >> 4
    lax.fori_loop(units, blocks * (BLOCK // UNIT), lambda p, c: (start(0, p), c)[1], 0)
    return blocks


def gathered_block(states_ref, packed_ref, sem):
    return pltpu.make_async_copy(states_ref.at[pl.ds(0, BLOCK)], packed_ref.at[pl.ds(0, BLOCK)], sem)


def pack_rows(counts_ref, values, packed_refs):
    me = lax.axis_index("rep")
    owners, cap = values[0].shape
    lane = lax.broadcasted_iota(jnp.int32, (1, cap), 1)
    for ref in packed_refs:
        ref[...] = jnp.zeros_like(ref)
    start = jnp.int32(0)
    for o in range(owners):
        count = counts_ref[o, me]
        row, shift = start >> 7, start & 127
        for value, ref in zip(values, packed_refs):
            kept = jnp.where(lane < count, value[o : o + 1, :], 0.0)
            turned = pltpu.roll(kept, shift, 1)
            ref[pl.ds(row, 1), :] += jnp.where(lane >= shift, turned, 0.0)
            ref[pl.ds(row + 1, 1), :] += jnp.where(lane < shift, turned, 0.0)
        start = start + units_of(count) * UNIT


def next_kernel(
    buffer_ref, w_in_ref, w_out_ref, fetch_ref, picked_ref, w_ref, rows_ref, w_second, fetch, total,
    sems, small_sems,
):
    steps = sems.shape[1]
    depth = w_in_ref.shape[0] // steps
    copies = []
    for i in range(steps):
        part = pl.ds(i * depth, depth)
        pair = (
            pltpu.make_async_copy(w_in_ref.at[part], w_ref.at[part], sems.at[0, i]),
            pltpu.make_async_copy(buffer_ref.at[:, part], rows_ref.at[:, part], sems.at[1, i]),
        )
        for copy in pair:
            copy.start()
        copies.append(pair)
    second = pltpu.make_async_copy(w_out_ref, w_second, small_sems.at[0])
    wanted = pltpu.make_async_copy(fetch_ref, fetch, small_sems.at[1])
    second.start()
    wanted.start()
    for i in range(steps):
        for copy in copies[i]:
            copy.wait()
        part = pl.ds(i * depth, depth)
        term = jnp.dot(rows_ref[:, part], w_ref[part, :], preferred_element_type=F32)
        total[...] = term if i == 0 else total[...] + term
    preact = total[...]
    hidden = low(preact * jax.nn.sigmoid(preact))
    second.wait()
    wanted.wait()
    logits = jnp.dot(hidden, w_second[...], preferred_element_type=F32)
    best = jax.nn.sigmoid(jnp.max(logits, axis=1, keepdims=True))
    halves = [jnp.broadcast_to(best[i : i + 128], (128, 128)).T[:8] for i in (0, 128)]
    for i in range(0, fetch.shape[0], 8):
        rows = fetch[pl.ds(i, 8), :]
        found = [
            jnp.take_along_axis(half, rows & 127, axis=1, mode="promise_in_bounds")
            for half in halves
        ]
        picked = jnp.where(rows < 128, found[0], found[1])
        for d in range(picked_ref.shape[0]):
            picked_ref[d, pl.ds(i, 8), :] = picked


def member_kernel(
    counts_ref, states_ref, w_first, w_second, table_ref, best_ref,
    actions_ref, rewards_ref, terminal_ref, returns_ref,
    targets_ref, packed_ref, d_hidden_ref, grad_ref, blocks_ref,
    preacts, target_row, scale_row, act_row, sems,
):
    me = lax.axis_index("rep")
    owners, cap = rewards_ref.shape
    blocks = gathered(counts_ref, states_ref, packed_ref, lambda b: sems.at[b])

    def arrived(b):
        gathered_block(states_ref, packed_ref, sems.at[b]).wait()

    def begin(b):
        part = pl.ds(pl.multiple_of(b * BLOCK, BLOCK), BLOCK)
        preacts[b & 1] = jnp.dot(packed_ref[part, :], w_first[...], preferred_element_type=F32)

    arrived(0)
    begin(jnp.int32(0))
    blocks_ref[...] = jnp.full(blocks_ref.shape, blocks, jnp.int32)
    counts = table_ref[...]
    counted = jnp.sum(counts).astype(F32)
    requester = lax.broadcasted_iota(jnp.int32, counts.shape, 1)
    mine = jnp.sum(jnp.where(requester == me, counts, 0), axis=1, keepdims=True)
    used = (lax.broadcasted_iota(jnp.int32, (owners, cap), 1) < mine).astype(F32)
    bootstrap = jnp.maximum(jnp.min(best_ref[...], axis=0), returns_ref[...])
    target = rewards_ref[...] + 0.98 * (1.0 - terminal_ref[...].astype(F32)) * bootstrap
    targets_ref[...] = used * target
    scale = used * 2.0 * (jnp.full((owners, cap), 65536.0, F32) / counted)
    pack_rows(
        counts_ref, [target, scale, high(actions_ref[...])], [target_row, scale_row, act_row]
    )
    grad_ref[...] = jnp.zeros_like(grad_ref)
    bins = lax.broadcasted_iota(jnp.int32, (grad_ref.shape[1], BLOCK), 0).astype(F32)
    w_out = w_second[...]
    w_out_turned = w_out.T

    def finish(b):
        at = pl.ds(pl.multiple_of(b * BLOCK, BLOCK), BLOCK)
        goal, scaled, acts = [
            jnp.concatenate([ref[pl.ds(2 * b + i, 1), :] for i in (0, 1)], axis=1)
            for ref in (target_row, scale_row, act_row)
        ]
        preact = preacts[b & 1].T
        sigmoid_pre = jax.nn.sigmoid(preact)
        hidden = low(preact * sigmoid_pre)
        logits = jnp.dot(w_out_turned, hidden, preferred_element_type=F32)
        chosen = bins == acts
        taken = jax.nn.sigmoid(jnp.sum(jnp.where(chosen, logits, 0.0), axis=0, keepdims=True))
        errors = (taken - goal) * taken * (1.0 - taken) * scaled
        d_logits = low(jnp.where(chosen, errors, 0.0))
        grad_ref[...] += lax.dot_general(
            hidden, d_logits, (((1,), (1,)), ((), ())), preferred_element_type=F32
        )
        back = jnp.dot(w_out, d_logits, preferred_element_type=F32)
        d_hidden_ref[:, at] = low(back * sigmoid_pre * (1.0 + preact * (1.0 - sigmoid_pre)))

    def step(b, carry):
        arrived(b)
        finish(b - 1)
        begin(b)
        return carry

    lax.fori_loop(1, blocks, step, 0)
    finish(blocks - 1)


def piece_kernel(steps, parts, with_recv, blocks_ref, d_hidden_ref, states_ref, grad_ref, *rest):
    recv_ref = rest[0] if with_recv else None
    out_refs, total = rest[with_recv:-1], rest[-1]
    me = lax.axis_index("rep")
    y, x, core = me >> 3, (me >> 1) & 3, me & 1
    blocks = blocks_ref[0, 0]
    width, depth = d_hidden_ref.shape[0], total.shape[2]
    rows = grad_ref.shape[0] // 16
    ats = [place(y ^ dy, (x + dx) & 3, core ^ dc) for dy, dx, dc in steps]

    for count in range(1, d_hidden_ref.shape[1] // BLOCK + 1):

        @pl.when(blocks == count)
        def _(deep=count * BLOCK):
            def piece(j, carry):
                at = ats[-1]
                for k in range(len(ats) - 1):
                    at = jnp.where(j == k, ats[k], at)
                columns = pl.ds(pl.multiple_of(at * depth, depth), depth)
                total[j, pl.ds(0, width), :] = jnp.dot(
                    d_hidden_ref[:, :deep], states_ref[:deep, columns], preferred_element_type=F32
                )
                return carry

            lax.fori_loop(0, len(ats), piece, 0)

    for j, at in enumerate(ats):
        total[j, pl.ds(width, rows), :] = grad_ref[pl.ds(pl.multiple_of(at * rows, rows), rows), :]
    if parts is None:
        out_refs[0][...] = low(total[...])
        return
    for out, (j, first, last, _) in zip(out_refs, parts):
        part = pl.ds(first, last - first)
        out[...] = (total[j, part, :] + high(recv_ref[j, part, :])).astype(out.dtype)


def final_kernel(own_ref, far_ref, first_ref, second_ref):
    width = first_ref.shape[1]
    total = own_ref[...] + high(far_ref[...])
    first_ref[...] = total[:width].T
    second_ref[...] = total[width:]


def update(
    cur_states, buffer, fetch_rows, fetch_counts, actions, rewards, terminal, mc_return, w_in, w_out
):
    w_first, w_second = w_in[0], w_out[0]
    owners, cap = fetch_rows.shape[1:]
    slots, model = cur_states.shape
    width, bins = w_second.shape
    members = lax.axis_size("ens")
    grid = lambda a: a.reshape(owners, cap)

    picked, w_kept = call(
        next_kernel,
        [pltpu.VMEM((members, owners, cap), F32), pltpu.VMEM(w_first.shape, BF16)],
        [HBM] * 4,
        [
            pltpu.VMEM(buffer.shape, BF16),
            pltpu.VMEM(w_second.shape, BF16),
            pltpu.VMEM((owners, cap), jnp.int32),
            pltpu.VMEM((buffer.shape[0], width), F32),
            pltpu.SemaphoreType.DMA((2, 8)),
            pltpu.SemaphoreType.DMA((2,)),
        ],
        flops=2 * buffer.shape[0] * model * width,
        bytes_moved=6 << 20,
    )(*[in_hbm(a) for a in (buffer, w_first, w_second, fetch_rows[0])])
    best = lax.all_to_all(
        picked.reshape(members * owners, 1, cap), ("ens", "rep"), 0, 0, tiled=True
    ).reshape(members, owners, cap)

    targets, packed, d_hidden, grad_second, blocks = call(
        member_kernel,
        [
            shape((owners, cap)),
            pltpu.VMEM((slots, model), BF16),
            pltpu.VMEM((width, slots), BF16),
            pltpu.VMEM((width, bins), F32),
            pltpu.VMEM((8, 128), jnp.int32),
        ],
        [SMEM, HBM] + [VMEM] * 8,
        [pltpu.VMEM((2, BLOCK, width), F32)]
        + [pltpu.VMEM((owners + 8, cap), F32)] * 3
        + [pltpu.SemaphoreType.DMA((slots // BLOCK,))],
        flops=slots * model * width,
        bytes_moved=14 << 20,
    )(
        fetch_counts, in_hbm(cur_states), w_kept, w_second, fetch_counts, best,
        grid(actions), grid(rewards), grid(terminal), grid(mc_return),
    )

    depth = model // 16
    tall = width + width // 16

    def pieces(steps, parts=None, recv=None):
        out = (
            shape((len(steps), tall, depth), BF16)
            if parts is None
            else [shape((last - first, depth), dtype) for _, first, last, dtype in parts]
        )
        extra = () if recv is None else (recv,)
        core = 0 if extra else 1
        return call(
            functools.partial(piece_kernel, [(*s, core) for s in steps], parts, len(extra)),
            out,
            [VMEM] * (4 + len(extra)),
            [pltpu.VMEM((len(steps), tall, depth), F32)],
            flops=len(steps) * slots * width * depth,
            bytes_moved=len(steps) << 18,
        )(blocks, d_hidden, packed, grad_second, *extra)

    other = [(1, 2), (1, 1), (1, 3)]
    same = [(0, 2), (0, 1), (0, 3)]
    own = [(1, 0), (0, 0)]

    away_other = sent(pieces(other), CORE)
    away_same = sent(pieces(same), CORE)
    far_other, right_other, left_other = pieces(
        other, [(j, 0, tall, BF16) for j in range(3)], away_other
    )
    across_far = sent(far_other, ACROSS)
    from_left_other = sent(right_other, RIGHT)
    from_right_other = sent(left_other, LEFT)
    away_own = sent(pieces(own), CORE)
    far_same, right_same, left_same = pieces(
        same, [(j, 0, tall, dtype) for j, dtype in enumerate((F32, BF16, BF16))], away_same
    )
    from_left_same = sent(right_same, RIGHT)
    from_right_same = sent(left_same, LEFT)
    own_other, own_same = pieces(own, [(j, 0, tall, F32) for j in range(2)], away_own)
    far_same, own_other, own_same = after(far_same, own_other, own_same)
    from_far = sent(low(far_same + high(across_far)), FAR)
    own_other = own_other + high(from_left_other) + high(from_right_other)
    over = sent(low(own_other), ACROSS)
    own_same = own_same + high(from_left_same) + high(from_right_same) + high(over)
    own_same, from_far = after(own_same, from_far)
    first, second = call(
        final_kernel, [shape((depth, width)), shape((width // 16, bins))], [VMEM] * 2
    )(own_same, from_far)
    return (targets.reshape(-1), first[None], second[None])


def solution(mesh):
    placed = (
        P("rep", None),
        P("rep", None),
        P("rep", None, None),
        P(),
        P("rep"),
        P("rep"),
        P("rep"),
        P("rep"),
        P("ens", None, None),
        P("ens", None, None),
    )
    return jax.shard_map(
        update,
        mesh=mesh,
        in_specs=placed,
        out_specs=(P("rep"), P("ens", "rep", None), P("ens", "rep", None)),
        check_vma=False,
    )
```

```python
import functools

import jax
import jax.numpy as jnp
from jax import lax
from jax.experimental import pallas as pl
from jax.experimental.pallas import tpu as pltpu
from jax.sharding import PartitionSpec as P


UNIT = 16
BLOCK = 256
F32, BF16 = jnp.float32, jnp.bfloat16
VMEM = pl.BlockSpec(memory_space=pltpu.VMEM)
SMEM = pl.BlockSpec(memory_space=pltpu.SMEM)
HBM = pl.BlockSpec(memory_space=pltpu.HBM)


def place(y, x, core):
    return y * 8 + x * 2 + core


def moves(fn):
    return [
        (place(y, x, c), place(*fn(y, x, c)))
        for y in range(2)
        for x in range(4)
        for c in range(2)
    ]


CORE = moves(lambda y, x, c: (y, x, 1 - c))
RIGHT = moves(lambda y, x, c: (y, (x + 1) % 4, c))
LEFT = moves(lambda y, x, c: (y, (x + 3) % 4, c))
FAR = moves(lambda y, x, c: (y, (x + 2) % 4, c))
ACROSS = moves(lambda y, x, c: (1 - y, x, c))


def sent(value, pairs):
    return lax.ppermute(value, "rep", pairs)


def low(value):
    return value.astype(BF16)


def high(value):
    return value.astype(F32)


def after(value, *others):
    return lax.optimization_barrier((value, *others))


def call(
    kernel, out_shape, in_specs, scratch=(), out_specs=None, limit=16, flops=0,
    bytes_moved=1 << 20,
):
    single = not isinstance(out_shape, (list, tuple))
    if out_specs is None:
        out_specs = VMEM if single else [VMEM] * len(out_shape)
    return pl.pallas_call(
        kernel,
        out_shape=out_shape,
        in_specs=in_specs,
        out_specs=out_specs,
        scratch_shapes=list(scratch),
        compiler_params=pltpu.CompilerParams(vmem_limit_bytes=limit << 20),
        cost_estimate=pl.CostEstimate(
            flops=flops, bytes_accessed=bytes_moved, transcendentals=0
        ),
    )


def in_hbm(array):
    return pltpu.with_memory_space_constraint(array, pltpu.HBM)


def shape(dims, dtype=F32):
    return jax.ShapeDtypeStruct(dims, dtype)


def units_of(count):
    return (count + (UNIT - 1)) >> 4


def run_copy(table, states_ref, packed_ref, sem, position):
    source = pl.multiple_of(table[0, position] * UNIT, UNIT)
    target = pl.multiple_of(position * UNIT, UNIT)
    return pltpu.make_async_copy(
        states_ref.at[pl.ds(source, UNIT)],
        packed_ref.at[pl.ds(target, UNIT)],
        sem,
    )


def listed(counts, table, start_first):
    me = lax.axis_index("rep")
    owners = counts.shape[0]
    runs = table.shape[1] // owners
    per_block = BLOCK // UNIT

    def put(source, position):
        table[0, position] = source

        @pl.when(position < per_block)
        def _():
            start_first(position)

    def owner(o, position):
        count = counts[o, me]
        table[1, o] = count

        def unit(u, position):
            put(o * runs + u, position)
            return position + 1

        return lax.fori_loop(0, units_of(count), unit, position)

    units = lax.fori_loop(0, owners, owner, jnp.int32(0))
    blocks = (units + (per_block - 1)) >> 4
    lax.fori_loop(units, blocks * per_block, lambda p, c: (put(0, p), c)[1], 0)
    table[1, owners] = blocks


def gathered_block(states_ref, packed_ref, sem):
    return pltpu.make_async_copy(states_ref.at[pl.ds(0, BLOCK)], packed_ref.at[pl.ds(0, BLOCK)], sem)


def pack_rows(table, values, packed_refs):
    owners, cap = values[0].shape
    lane = lax.broadcasted_iota(jnp.int32, (1, cap), 1)
    for ref in packed_refs:
        ref[...] = jnp.zeros_like(ref)
    start = jnp.int32(0)
    for o in range(owners):
        count = table[1, o]
        row, shift = start >> 7, start & 127
        for value, ref in zip(values, packed_refs):
            kept = jnp.where(lane < count, value[o : o + 1, :], 0.0)
            turned = pltpu.roll(kept, shift, 1)
            ref[pl.ds(row, 1), :] += jnp.where(lane >= shift, turned, 0.0)
            ref[pl.ds(row + 1, 1), :] += jnp.where(lane < shift, turned, 0.0)
        start = start + units_of(count) * UNIT


def next_kernel(
    buffer_ref, w_in_ref, w_out_ref, fetch_ref, counts_ref, states_ref,
    picked_ref, w_ref, first_ref, table_ref,
    rows_ref, w_second, fetch, total, counts, table, sems, small_sems,
):
    steps = sems.shape[1]
    depth = w_in_ref.shape[0] // steps
    counted = pltpu.make_async_copy(counts_ref, counts, small_sems.at[2])
    counted.start()
    copies = []
    for i in range(steps):
        part = pl.ds(i * depth, depth)
        pair = (
            pltpu.make_async_copy(w_in_ref.at[part], w_ref.at[part], sems.at[0, i]),
            pltpu.make_async_copy(buffer_ref.at[:, part], rows_ref.at[:, part], sems.at[1, i]),
        )
        for copy in pair:
            copy.start()
        copies.append(pair)
    second = pltpu.make_async_copy(w_out_ref, w_second, small_sems.at[0])
    wanted = pltpu.make_async_copy(fetch_ref, fetch, small_sems.at[1])
    second.start()
    wanted.start()
    counted.wait()
    listed(
        counts,
        table,
        lambda p: run_copy(table, states_ref, first_ref, small_sems.at[3], p).start(),
    )
    kept_table = pltpu.make_async_copy(table, table_ref, small_sems.at[2])
    kept_table.start()
    for i in range(steps):
        for copy in copies[i]:
            copy.wait()
        part = pl.ds(i * depth, depth)
        term = jnp.dot(rows_ref[:, part], w_ref[part, :], preferred_element_type=F32)
        total[...] = term if i == 0 else total[...] + term
    preact = total[...]
    hidden = low(preact * jax.nn.sigmoid(preact))
    second.wait()
    wanted.wait()
    logits = jnp.dot(hidden, w_second[...], preferred_element_type=F32)
    best = jax.nn.sigmoid(jnp.max(logits, axis=1, keepdims=True))
    halves = [jnp.broadcast_to(best[i : i + 128], (128, 128)).T[:8] for i in (0, 128)]
    for i in range(0, fetch.shape[0], 8):
        rows = fetch[pl.ds(i, 8), :]
        found = [
            jnp.take_along_axis(half, rows & 127, axis=1, mode="promise_in_bounds")
            for half in halves
        ]
        picked = jnp.where(rows < 128, found[0], found[1])
        for d in range(picked_ref.shape[0]):
            picked_ref[d, pl.ds(i, 8), :] = picked
    kept_table.wait()
    gathered_block(states_ref, first_ref, small_sems.at[3]).wait()


def member_kernel(
    listed_ref, first_ref, states_ref, w_first, w_second, table_ref, best_ref,
    actions_ref, rewards_ref, terminal_ref, returns_ref,
    targets_ref, packed_ref, d_hidden_ref, grad_ref, blocks_ref,
    raw, turned, slope, hidden_now, target_row, scale_row, act_row, table, sems, start_sems,
):
    me = lax.axis_index("rep")
    owners, cap = rewards_ref.shape
    load = pltpu.make_async_copy(listed_ref, table, start_sems.at[0])
    load.start()
    place_first = pltpu.make_async_copy(
        first_ref, packed_ref.at[pl.ds(0, BLOCK)], start_sems.at[1]
    )
    load.wait()
    blocks = table[1, owners]

    def fetch(b):
        @pl.when(b < blocks)
        def _():
            for i in range(BLOCK // UNIT):
                run_copy(
                    table, states_ref, packed_ref, sems.at[b], b * (BLOCK // UNIT) + i
                ).start()

    fetch(jnp.int32(1))
    fetch(jnp.int32(2))
    place_first.start()

    def arrived(b):
        gathered_block(states_ref, packed_ref, sems.at[b]).wait()

    half = w_first.shape[1] // 2
    halves = (pl.ds(0, half), pl.ds(half, half))

    def begin(b, part):
        rows = pl.ds(pl.multiple_of(b * BLOCK, BLOCK), BLOCK)
        raw[:, part] = jnp.dot(packed_ref[rows, :], w_first[:, part], preferred_element_type=F32)

    def turn(part):
        turned[part, :] = raw[:, part].T

    for part in halves:
        raw[:, part] = jnp.dot(first_ref[...], w_first[:, part], preferred_element_type=F32)
        turn(part)
    blocks_ref[...] = jnp.full(blocks_ref.shape, blocks, jnp.int32)
    counts = table_ref[...]
    counted = jnp.sum(counts).astype(F32)
    requester = lax.broadcasted_iota(jnp.int32, counts.shape, 1)
    mine = jnp.sum(jnp.where(requester == me, counts, 0), axis=1, keepdims=True)
    used = (lax.broadcasted_iota(jnp.int32, (owners, cap), 1) < mine).astype(F32)
    bootstrap = jnp.maximum(jnp.min(best_ref[...], axis=0), returns_ref[...])
    target = rewards_ref[...] + 0.98 * (1.0 - terminal_ref[...].astype(F32)) * bootstrap
    targets_ref[...] = used * target
    scale = used * 2.0 * (jnp.full((owners, cap), 65536.0, F32) / counted)
    pack_rows(
        table, [target, scale, high(actions_ref[...])], [target_row, scale_row, act_row]
    )
    grad_ref[...] = jnp.zeros_like(grad_ref)
    bins = lax.broadcasted_iota(jnp.int32, (grad_ref.shape[1], BLOCK), 0).astype(F32)
    w_out = w_second[...]
    w_out_turned = w_out.T

    def finish(b, following=None):
        at = pl.ds(pl.multiple_of(b * BLOCK, BLOCK), BLOCK)
        goal, scaled, acts = [
            jnp.concatenate([ref[pl.ds(2 * b + i, 1), :] for i in (0, 1)], axis=1)
            for ref in (target_row, scale_row, act_row)
        ]
        preact = turned[...]
        sigmoid_pre = jax.nn.sigmoid(preact)
        hidden_now[...] = low(preact * sigmoid_pre)
        slope[...] = sigmoid_pre * (1.0 + preact * (1.0 - sigmoid_pre))
        if following is not None:
            begin(following, halves[0])
        hidden = hidden_now[...]
        logits = jnp.dot(w_out_turned, hidden, preferred_element_type=F32)
        if following is not None:
            begin(following, halves[1])
            turn(halves[0])
        chosen = bins == acts
        taken = jax.nn.sigmoid(jnp.sum(jnp.where(chosen, logits, 0.0), axis=0, keepdims=True))
        errors = (taken - goal) * taken * (1.0 - taken) * scaled
        d_logits = low(jnp.where(chosen, errors, 0.0))
        grad_ref[...] += lax.dot_general(
            hidden, d_logits, (((1,), (1,)), ((), ())), preferred_element_type=F32
        )
        back = jnp.dot(w_out, d_logits, preferred_element_type=F32)
        d_hidden_ref[:, at] = low(back * slope[...])
        if following is not None:
            turn(halves[1])

    def step(b, carry):
        arrived(b)
        fetch(b + 2)
        finish(b - 1, b)
        return carry

    lax.fori_loop(1, blocks, step, 0)
    finish(blocks - 1)
    place_first.wait()


def piece_kernel(steps, parts, with_recv, blocks_ref, d_hidden_ref, states_ref, grad_ref, *rest):
    recv_ref = rest[0] if with_recv else None
    out_refs, total = rest[with_recv:-1], rest[-1]
    me = lax.axis_index("rep")
    y, x, core = me >> 3, (me >> 1) & 3, me & 1
    blocks = blocks_ref[0, 0]
    width, depth = d_hidden_ref.shape[0], total.shape[2]
    rows = grad_ref.shape[0] // 16
    ats = [place(y ^ dy, (x + dx) & 3, core ^ dc) for dy, dx, dc in steps]

    for count in range(1, d_hidden_ref.shape[1] // BLOCK + 1):

        @pl.when(blocks == count)
        def _(deep=count * BLOCK):
            def piece(j, carry):
                at = ats[-1]
                for k in range(len(ats) - 1):
                    at = jnp.where(j == k, ats[k], at)
                columns = pl.ds(pl.multiple_of(at * depth, depth), depth)
                total[j, pl.ds(0, width), :] = jnp.dot(
                    d_hidden_ref[:, :deep], states_ref[:deep, columns], preferred_element_type=F32
                )
                return carry

            lax.fori_loop(0, len(ats), piece, 0)

    for j, at in enumerate(ats):
        total[j, pl.ds(width, rows), :] = grad_ref[pl.ds(pl.multiple_of(at * rows, rows), rows), :]
    if parts is None:
        out_refs[0][...] = low(total[...])
        return
    for out, (j, first, last, _) in zip(out_refs, parts):
        part = pl.ds(first, last - first)
        out[...] = (total[j, part, :] + high(recv_ref[j, part, :])).astype(out.dtype)


def final_kernel(own_ref, far_ref, first_ref, second_ref):
    width = first_ref.shape[1]
    total = own_ref[...] + high(far_ref[...])
    first_ref[...] = total[:width].T
    second_ref[...] = total[width:]


def update(
    cur_states, buffer, fetch_rows, fetch_counts, actions, rewards, terminal, mc_return, w_in, w_out
):
    w_first, w_second = w_in[0], w_out[0]
    owners, cap = fetch_rows.shape[1:]
    slots, model = cur_states.shape
    width, bins = w_second.shape
    members = lax.axis_size("ens")
    grid = lambda a: a.reshape(owners, cap)

    picked, w_kept, first_block, table = call(
        next_kernel,
        [
            pltpu.VMEM((members, owners, cap), F32),
            pltpu.VMEM(w_first.shape, BF16),
            pltpu.VMEM((BLOCK, model), BF16),
            pltpu.VMEM((8, slots // UNIT), jnp.int32),
        ],
        [HBM] * 6,
        [
            pltpu.VMEM(buffer.shape, BF16),
            pltpu.VMEM(w_second.shape, BF16),
            pltpu.VMEM((owners, cap), jnp.int32),
            pltpu.VMEM((buffer.shape[0], width), F32),
            pltpu.SMEM(fetch_counts.shape, jnp.int32),
            pltpu.SMEM((8, slots // UNIT), jnp.int32),
            pltpu.SemaphoreType.DMA((2, 8)),
            pltpu.SemaphoreType.DMA((4,)),
        ],
        flops=2 * buffer.shape[0] * model * width,
        bytes_moved=6 << 20,
    )(
        *[
            in_hbm(a)
            for a in (buffer, w_first, w_second, fetch_rows[0], fetch_counts, cur_states)
        ]
    )
    best = lax.all_to_all(
        picked.reshape(members * owners, 1, cap), ("ens", "rep"), 0, 0, tiled=True
    ).reshape(members, owners, cap)

    targets, packed, d_hidden, grad_second, blocks = call(
        member_kernel,
        [
            shape((owners, cap)),
            pltpu.VMEM((slots, model), BF16),
            pltpu.VMEM((width, slots), BF16),
            pltpu.VMEM((width, bins), F32),
            pltpu.VMEM((8, 128), jnp.int32),
        ],
        [VMEM, VMEM, HBM] + [VMEM] * 8,
        [pltpu.VMEM((BLOCK, width), F32)]
        + [pltpu.VMEM((width, BLOCK), F32)] * 2
        + [pltpu.VMEM((width, BLOCK), BF16)]
        + [pltpu.VMEM((owners + 8, cap), F32)] * 3
        + [pltpu.SMEM((8, slots // UNIT), jnp.int32)]
        + [pltpu.SemaphoreType.DMA((slots // BLOCK,)), pltpu.SemaphoreType.DMA((2,))],
        flops=slots * model * width,
        bytes_moved=14 << 20,
    )(
        table, first_block, in_hbm(cur_states), w_kept, w_second, fetch_counts, best,
        grid(actions), grid(rewards), grid(terminal), grid(mc_return),
    )

    depth = model // 16
    tall = width + width // 16

    def pieces(steps, parts=None, recv=None):
        out = (
            shape((len(steps), tall, depth), BF16)
            if parts is None
            else [shape((last - first, depth), dtype) for _, first, last, dtype in parts]
        )
        extra = () if recv is None else (recv,)
        core = 0 if extra else 1
        return call(
            functools.partial(piece_kernel, [(*s, core) for s in steps], parts, len(extra)),
            out,
            [VMEM] * (4 + len(extra)),
            [pltpu.VMEM((len(steps), tall, depth), F32)],
            flops=len(steps) * slots * width * depth,
            bytes_moved=len(steps) << 18,
        )(blocks, d_hidden, packed, grad_second, *extra)

    other = [(1, 2), (1, 1), (1, 3)]
    same = [(0, 2), (0, 1), (0, 3)]
    own = [(1, 0), (0, 0)]

    away_other = sent(pieces(other), CORE)
    away_same = sent(pieces(same), CORE)
    far_other, right_other, left_other = pieces(
        other, [(j, 0, tall, BF16) for j in range(3)], away_other
    )
    across_far = sent(far_other, ACROSS)
    from_left_other = sent(right_other, RIGHT)
    from_right_other = sent(left_other, LEFT)
    away_own = sent(pieces(own), CORE)
    far_same, right_same, left_same = pieces(
        same, [(j, 0, tall, dtype) for j, dtype in enumerate((F32, BF16, BF16))], away_same
    )
    from_left_same = sent(right_same, RIGHT)
    from_right_same = sent(left_same, LEFT)
    own_other, own_same = pieces(own, [(j, 0, tall, F32) for j in range(2)], away_own)
    far_same, own_other, own_same = after(far_same, own_other, own_same)
    from_far = sent(low(far_same + high(across_far)), FAR)
    own_other = own_other + high(from_left_other) + high(from_right_other)
    over = sent(low(own_other), ACROSS)
    own_same = own_same + high(from_left_same) + high(from_right_same) + high(over)
    own_same, from_far = after(own_same, from_far)
    first, second = call(
        final_kernel, [shape((depth, width)), shape((width // 16, bins))], [VMEM] * 2
    )(own_same, from_far)
    return (targets.reshape(-1), first[None], second[None])


def solution(mesh):
    placed = (
        P("rep", None),
        P("rep", None),
        P("rep", None, None),
        P(),
        P("rep"),
        P("rep"),
        P("rep"),
        P("rep"),
        P("ens", None, None),
        P("ens", None, None),
    )
    return jax.shard_map(
        update,
        mesh=mesh,
        in_specs=placed,
        out_specs=(P("rep"), P("ens", "rep", None), P("ens", "rep", None)),
        check_vma=False,
    )
```

```python
import functools

import jax
import jax.numpy as jnp
from jax import lax
from jax.experimental import pallas as pl
from jax.experimental.pallas import tpu as pltpu
from jax.sharding import PartitionSpec as P


UNIT = 16
BLOCK = 256
F32, BF16 = jnp.float32, jnp.bfloat16
VMEM = pl.BlockSpec(memory_space=pltpu.VMEM)
SMEM = pl.BlockSpec(memory_space=pltpu.SMEM)
HBM = pl.BlockSpec(memory_space=pltpu.HBM)


def place(y, x, core):
    return y * 8 + x * 2 + core


def moves(fn):
    return [
        (place(y, x, c), place(*fn(y, x, c)))
        for y in range(2)
        for x in range(4)
        for c in range(2)
    ]


CORE = moves(lambda y, x, c: (y, x, 1 - c))
RIGHT = moves(lambda y, x, c: (y, (x + 1) % 4, c))
LEFT = moves(lambda y, x, c: (y, (x + 3) % 4, c))
FAR = moves(lambda y, x, c: (y, (x + 2) % 4, c))
ACROSS = moves(lambda y, x, c: (1 - y, x, c))


def sent(value, pairs):
    return lax.ppermute(value, "rep", pairs)


def low(value):
    return value.astype(BF16)


def high(value):
    return value.astype(F32)


def after(value, *others):
    return lax.optimization_barrier((value, *others))


def call(
    kernel, out_shape, in_specs, scratch=(), out_specs=None, limit=16, flops=0,
    bytes_moved=1 << 20,
):
    single = not isinstance(out_shape, (list, tuple))
    if out_specs is None:
        out_specs = VMEM if single else [VMEM] * len(out_shape)
    return pl.pallas_call(
        kernel,
        out_shape=out_shape,
        in_specs=in_specs,
        out_specs=out_specs,
        scratch_shapes=list(scratch),
        compiler_params=pltpu.CompilerParams(vmem_limit_bytes=limit << 20),
        cost_estimate=pl.CostEstimate(
            flops=flops, bytes_accessed=bytes_moved, transcendentals=0
        ),
    )


def in_hbm(array):
    return pltpu.with_memory_space_constraint(array, pltpu.HBM)


def shape(dims, dtype=F32):
    return jax.ShapeDtypeStruct(dims, dtype)


def units_of(count):
    return (count + (UNIT - 1)) >> 4


def run_copy(table, states_ref, packed_ref, sem, position):
    source = pl.multiple_of(table[0, position] * UNIT, UNIT)
    target = pl.multiple_of(position * UNIT, UNIT)
    return pltpu.make_async_copy(
        states_ref.at[pl.ds(source, UNIT)],
        packed_ref.at[pl.ds(target, UNIT)],
        sem,
    )


def listed(counts, table, start_first):
    me = lax.axis_index("rep")
    owners = counts.shape[0]
    runs = table.shape[1] // owners
    per_block = BLOCK // UNIT

    def put(source, position):
        table[0, position] = source

        @pl.when(position < per_block)
        def _():
            start_first(position)

    def owner(o, position):
        count = counts[o, me]
        table[1, o] = count

        def unit(u, position):
            put(o * runs + u, position)
            return position + 1

        return lax.fori_loop(0, units_of(count), unit, position)

    units = lax.fori_loop(0, owners, owner, jnp.int32(0))
    blocks = (units + (per_block - 1)) >> 4
    lax.fori_loop(units, blocks * per_block, lambda p, c: (put(0, p), c)[1], 0)
    table[1, owners] = blocks


def gathered_block(states_ref, packed_ref, sem):
    return pltpu.make_async_copy(states_ref.at[pl.ds(0, BLOCK)], packed_ref.at[pl.ds(0, BLOCK)], sem)


def pack_rows(table, values, packed_refs):
    owners, cap = values[0].shape
    lane = lax.broadcasted_iota(jnp.int32, (1, cap), 1)
    for ref in packed_refs:
        ref[...] = jnp.zeros_like(ref)
    start = jnp.int32(0)
    for o in range(owners):
        count = table[1, o]
        row, shift = start >> 7, start & 127
        for value, ref in zip(values, packed_refs):
            kept = jnp.where(lane < count, value[o : o + 1, :], 0.0)
            turned = pltpu.roll(kept, shift, 1)
            ref[pl.ds(row, 1), :] += jnp.where(lane >= shift, turned, 0.0)
            ref[pl.ds(row + 1, 1), :] += jnp.where(lane < shift, turned, 0.0)
        start = start + units_of(count) * UNIT


def next_kernel(
    buffer_ref, w_in_ref, w_out_ref, fetch_ref, counts_ref, states_ref,
    picked_ref, w_ref, first_ref, table,
    rows_ref, w_second, fetch, total, counts, sems, small_sems,
):
    steps = sems.shape[1]
    depth = w_in_ref.shape[0] // steps
    counted = pltpu.make_async_copy(counts_ref, counts, small_sems.at[2])
    counted.start()
    copies = []
    for i in range(steps):
        part = pl.ds(i * depth, depth)
        pair = (
            pltpu.make_async_copy(w_in_ref.at[part], w_ref.at[part], sems.at[0, i]),
            pltpu.make_async_copy(buffer_ref.at[:, part], rows_ref.at[:, part], sems.at[1, i]),
        )
        for copy in pair:
            copy.start()
        copies.append(pair)
    second = pltpu.make_async_copy(w_out_ref, w_second, small_sems.at[0])
    wanted = pltpu.make_async_copy(fetch_ref, fetch, small_sems.at[1])
    second.start()
    wanted.start()
    counted.wait()
    listed(
        counts,
        table,
        lambda p: run_copy(table, states_ref, first_ref, small_sems.at[3], p).start(),
    )
    for i in range(steps):
        for copy in copies[i]:
            copy.wait()
        part = pl.ds(i * depth, depth)
        term = jnp.dot(rows_ref[:, part], w_ref[part, :], preferred_element_type=F32)
        total[...] = term if i == 0 else total[...] + term
    preact = total[...]
    hidden = low(preact * jax.nn.sigmoid(preact))
    second.wait()
    wanted.wait()
    logits = jnp.dot(hidden, w_second[...], preferred_element_type=F32)
    best = jax.nn.sigmoid(jnp.max(logits, axis=1, keepdims=True))
    halves = [jnp.broadcast_to(best[i : i + 128], (128, 128)).T[:8] for i in (0, 128)]
    for i in range(0, fetch.shape[0], 8):
        rows = fetch[pl.ds(i, 8), :]
        found = [
            jnp.take_along_axis(half, rows & 127, axis=1, mode="promise_in_bounds")
            for half in halves
        ]
        picked = jnp.where(rows < 128, found[0], found[1])
        for d in range(picked_ref.shape[0]):
            picked_ref[d, pl.ds(i, 8), :] = picked
    gathered_block(states_ref, first_ref, small_sems.at[3]).wait()


def member_kernel(
    table, first_ref, states_ref, w_first, w_second, table_ref, best_ref,
    actions_ref, rewards_ref, terminal_ref, returns_ref,
    targets_ref, packed_ref, d_hidden_ref, grad_ref,
    raw, turned, slope, hidden_now, target_row, scale_row, act_row, sems, start_sems,
):
    me = lax.axis_index("rep")
    owners, cap = rewards_ref.shape
    place_first = pltpu.make_async_copy(
        first_ref, packed_ref.at[pl.ds(0, BLOCK)], start_sems.at[0]
    )
    blocks = table[1, owners]

    def fetch(b):
        @pl.when(b < blocks)
        def _():
            for i in range(BLOCK // UNIT):
                run_copy(
                    table, states_ref, packed_ref, sems.at[b], b * (BLOCK // UNIT) + i
                ).start()

    fetch(jnp.int32(1))
    fetch(jnp.int32(2))
    place_first.start()

    def arrived(b):
        gathered_block(states_ref, packed_ref, sems.at[b]).wait()

    half = w_first.shape[1] // 2
    halves = (pl.ds(0, half), pl.ds(half, half))

    def begin(b, part):
        rows = pl.ds(pl.multiple_of(b * BLOCK, BLOCK), BLOCK)
        raw[:, part] = jnp.dot(packed_ref[rows, :], w_first[:, part], preferred_element_type=F32)

    def turn(part):
        turned[part, :] = raw[:, part].T

    for part in halves:
        raw[:, part] = jnp.dot(first_ref[...], w_first[:, part], preferred_element_type=F32)
        turn(part)
    counts = table_ref[...]
    counted = jnp.sum(counts).astype(F32)
    requester = lax.broadcasted_iota(jnp.int32, counts.shape, 1)
    mine = jnp.sum(jnp.where(requester == me, counts, 0), axis=1, keepdims=True)
    used = (lax.broadcasted_iota(jnp.int32, (owners, cap), 1) < mine).astype(F32)
    bootstrap = jnp.maximum(jnp.min(best_ref[...], axis=0), returns_ref[...])
    target = rewards_ref[...] + 0.98 * (1.0 - terminal_ref[...].astype(F32)) * bootstrap
    targets_ref[...] = used * target
    scale = used * 2.0 * (jnp.full((owners, cap), 65536.0, F32) / counted)
    pack_rows(
        table, [target, scale, high(actions_ref[...])], [target_row, scale_row, act_row]
    )
    grad_ref[...] = jnp.zeros_like(grad_ref)
    bins = lax.broadcasted_iota(jnp.int32, (grad_ref.shape[1], BLOCK), 0).astype(F32)
    w_out = w_second[...]
    w_out_turned = w_out.T

    def finish(b, following=None):
        at = pl.ds(pl.multiple_of(b * BLOCK, BLOCK), BLOCK)
        goal, scaled, acts = [
            jnp.concatenate([ref[pl.ds(2 * b + i, 1), :] for i in (0, 1)], axis=1)
            for ref in (target_row, scale_row, act_row)
        ]
        preact = turned[...]
        sigmoid_pre = jax.nn.sigmoid(preact)
        hidden_now[...] = low(preact * sigmoid_pre)
        slope[...] = sigmoid_pre * (1.0 + preact * (1.0 - sigmoid_pre))
        if following is not None:
            begin(following, halves[0])
        hidden = hidden_now[...]
        logits = jnp.dot(w_out_turned, hidden, preferred_element_type=F32)
        if following is not None:
            begin(following, halves[1])
            turn(halves[0])
        chosen = bins == acts
        taken = jax.nn.sigmoid(jnp.sum(jnp.where(chosen, logits, 0.0), axis=0, keepdims=True))
        errors = (taken - goal) * taken * (1.0 - taken) * scaled
        d_logits = low(jnp.where(chosen, errors, 0.0))
        grad_ref[...] += lax.dot_general(
            hidden, d_logits, (((1,), (1,)), ((), ())), preferred_element_type=F32
        )
        back = jnp.dot(w_out, d_logits, preferred_element_type=F32)
        d_hidden_ref[:, at] = low(back * slope[...])
        if following is not None:
            turn(halves[1])

    def step(b, carry):
        arrived(b)
        fetch(b + 2)
        finish(b - 1, b)
        return carry

    lax.fori_loop(1, blocks, step, 0)
    finish(blocks - 1)
    place_first.wait()


def piece_kernel(steps, parts, with_recv, table, d_hidden_ref, states_ref, grad_ref, *rest):
    recv_ref = rest[0] if with_recv else None
    out_refs, total = (rest[1:-1], rest[-1]) if with_recv else (rest, rest[-1])
    me = lax.axis_index("rep")
    y, x, core = me >> 3, (me >> 1) & 3, me & 1
    blocks = table[1, 16]
    width, depth = d_hidden_ref.shape[0], total.shape[2]
    rows = grad_ref.shape[0] // 16
    first, second = pl.ds(0, width), pl.ds(width, rows)
    ats = [place(y ^ dy, (x + dx) & 3, core ^ dc) for dy, dx, dc in steps]

    for count in range(1, d_hidden_ref.shape[1] // BLOCK + 1):

        @pl.when(blocks == count)
        def _(deep=count * BLOCK):
            def piece(j, carry):
                at = ats[-1]
                for k in range(len(ats) - 1):
                    at = jnp.where(j == k, ats[k], at)
                columns = pl.ds(pl.multiple_of(at * depth, depth), depth)
                term = jnp.dot(
                    d_hidden_ref[:, :deep], states_ref[:deep, columns], preferred_element_type=F32
                )
                if with_recv:
                    term = term + high(recv_ref[j, first, :])
                total[j, first, :] = term.astype(total.dtype)
                return carry

            lax.fori_loop(0, len(ats), piece, 0)

    for j, at in enumerate(ats):
        term = grad_ref[pl.ds(pl.multiple_of(at * rows, rows), rows), :]
        if with_recv:
            term = term + high(recv_ref[j, second, :])
        total[j, second, :] = term.astype(total.dtype)
    for out, (j, start, stop, _) in zip(out_refs, parts or ()):
        out[...] = total[j, pl.ds(start, stop - start), :].astype(out.dtype)


def final_kernel(own_ref, far_ref, first_ref, second_ref):
    width = first_ref.shape[1]
    total = own_ref[...] + high(far_ref[...])
    first_ref[...] = total[:width].T
    second_ref[...] = total[width:]


def update(
    cur_states, buffer, fetch_rows, fetch_counts, actions, rewards, terminal, mc_return, w_in, w_out
):
    w_first, w_second = w_in[0], w_out[0]
    owners, cap = fetch_rows.shape[1:]
    slots, model = cur_states.shape
    width, bins = w_second.shape
    members = lax.axis_size("ens")
    grid = lambda a: a.reshape(owners, cap)

    picked, w_kept, first_block, table = call(
        next_kernel,
        [
            pltpu.VMEM((members, owners, cap), F32),
            pltpu.VMEM(w_first.shape, BF16),
            pltpu.VMEM((BLOCK, model), BF16),
            pltpu.SMEM((8, slots // UNIT), jnp.int32),
        ],
        [HBM] * 6,
        [
            pltpu.VMEM(buffer.shape, BF16),
            pltpu.VMEM(w_second.shape, BF16),
            pltpu.VMEM((owners, cap), jnp.int32),
            pltpu.VMEM((buffer.shape[0], width), F32),
            pltpu.SMEM(fetch_counts.shape, jnp.int32),
            pltpu.SemaphoreType.DMA((2, 8)),
            pltpu.SemaphoreType.DMA((4,)),
        ],
        flops=2 * buffer.shape[0] * model * width,
        bytes_moved=6 << 20,
        out_specs=[VMEM, VMEM, VMEM, SMEM],
    )(
        *[
            in_hbm(a)
            for a in (buffer, w_first, w_second, fetch_rows[0], fetch_counts, cur_states)
        ]
    )
    best = lax.all_to_all(
        picked.reshape(members * owners, 1, cap), ("ens", "rep"), 0, 0, tiled=True
    ).reshape(members, owners, cap)

    targets, packed, d_hidden, grad_second = call(
        member_kernel,
        [
            shape((owners, cap)),
            pltpu.VMEM((slots, model), BF16),
            pltpu.VMEM((width, slots), BF16),
            pltpu.VMEM((width, bins), F32),
        ],
        [SMEM, VMEM, HBM] + [VMEM] * 8,
        [pltpu.VMEM((BLOCK, width), F32)]
        + [pltpu.VMEM((width, BLOCK), F32)] * 2
        + [pltpu.VMEM((width, BLOCK), BF16)]
        + [pltpu.VMEM((owners + 8, cap), F32)] * 3
        + [pltpu.SemaphoreType.DMA((slots // BLOCK,)), pltpu.SemaphoreType.DMA((1,))],
        flops=slots * model * width,
        bytes_moved=14 << 20,
    )(
        table, first_block, in_hbm(cur_states), w_kept, w_second, fetch_counts, best,
        grid(actions), grid(rewards), grid(terminal), grid(mc_return),
    )

    depth = model // 16
    tall = width + width // 16

    def pieces(steps, parts=None, recv=None):
        out = (
            shape((len(steps), tall, depth), BF16)
            if parts is None
            else [shape((last - first, depth), dtype) for _, first, last, dtype in parts]
        )
        extra = () if recv is None else (recv,)
        core = 0 if extra else 1
        return call(
            functools.partial(piece_kernel, [(*s, core) for s in steps], parts, len(extra)),
            out,
            [SMEM] + [VMEM] * (3 + len(extra)),
            [pltpu.VMEM((len(steps), tall, depth), F32)] if extra else [],
            flops=len(steps) * slots * width * depth,
            bytes_moved=len(steps) << 18,
        )(table, d_hidden, packed, grad_second, *extra)

    other = [(1, 2), (1, 1), (1, 3)]
    same = [(0, 2), (0, 1), (0, 3)]
    own = [(1, 0), (0, 0)]

    away_other = sent(pieces(other), CORE)
    away_same = sent(pieces(same), CORE)
    far_other, right_other, left_other = pieces(
        other, [(j, 0, tall, BF16) for j in range(3)], away_other
    )
    across_far = sent(far_other, ACROSS)
    from_left_other = sent(right_other, RIGHT)
    from_right_other = sent(left_other, LEFT)
    away_own = sent(pieces(own), CORE)
    far_same, right_same, left_same = pieces(
        same, [(j, 0, tall, dtype) for j, dtype in enumerate((F32, BF16, BF16))], away_same
    )
    from_left_same = sent(right_same, RIGHT)
    from_right_same = sent(left_same, LEFT)
    own_other, own_same = pieces(own, [(j, 0, tall, F32) for j in range(2)], away_own)
    far_same, own_other, own_same = after(far_same, own_other, own_same)
    from_far = sent(low(far_same + high(across_far)), FAR)
    own_other = own_other + high(from_left_other) + high(from_right_other)
    over = sent(low(own_other), ACROSS)
    own_same = own_same + high(from_left_same) + high(from_right_same) + high(over)
    own_same, from_far = after(own_same, from_far)
    first, second = call(
        final_kernel, [shape((depth, width)), shape((width // 16, bins))], [VMEM] * 2
    )(own_same, from_far)
    return (targets.reshape(-1), first[None], second[None])


def solution(mesh):
    placed = (
        P("rep", None),
        P("rep", None),
        P("rep", None, None),
        P(),
        P("rep"),
        P("rep"),
        P("rep"),
        P("rep"),
        P("ens", None, None),
        P("ens", None, None),
    )
    return jax.shard_map(
        update,
        mesh=mesh,
        in_specs=placed,
        out_specs=(P("rep"), P("ens", "rep", None), P("ens", "rep", None)),
        check_vma=False,
    )
```

```python
import functools

import jax
import jax.numpy as jnp
from jax import lax
from jax.experimental import pallas as pl
from jax.experimental.pallas import tpu as pltpu
from jax.sharding import PartitionSpec as P


UNIT = 16
BLOCK = 256
F32, BF16 = jnp.float32, jnp.bfloat16
VMEM = pl.BlockSpec(memory_space=pltpu.VMEM)
SMEM = pl.BlockSpec(memory_space=pltpu.SMEM)
HBM = pl.BlockSpec(memory_space=pltpu.HBM)


def place(y, x, core):
    return y * 8 + x * 2 + core


def moves(fn):
    return [
        (place(y, x, c), place(*fn(y, x, c)))
        for y in range(2)
        for x in range(4)
        for c in range(2)
    ]


CORE = moves(lambda y, x, c: (y, x, 1 - c))
RIGHT = moves(lambda y, x, c: (y, (x + 1) % 4, c))
LEFT = moves(lambda y, x, c: (y, (x + 3) % 4, c))
FAR = moves(lambda y, x, c: (y, (x + 2) % 4, c))
ACROSS = moves(lambda y, x, c: (1 - y, x, c))


def sent(value, pairs):
    return lax.ppermute(value, "rep", pairs)


def low(value):
    return value.astype(BF16)


def high(value):
    return value.astype(F32)


def after(value, *others):
    return lax.optimization_barrier((value, *others))


def call(
    kernel, out_shape, in_specs, scratch=(), out_specs=None, limit=16, flops=0,
    bytes_moved=1 << 20,
):
    single = not isinstance(out_shape, (list, tuple))
    if out_specs is None:
        out_specs = VMEM if single else [VMEM] * len(out_shape)
    return pl.pallas_call(
        kernel,
        out_shape=out_shape,
        in_specs=in_specs,
        out_specs=out_specs,
        scratch_shapes=list(scratch),
        compiler_params=pltpu.CompilerParams(vmem_limit_bytes=limit << 20),
        cost_estimate=pl.CostEstimate(
            flops=flops, bytes_accessed=bytes_moved, transcendentals=0
        ),
    )


def in_hbm(array):
    return pltpu.with_memory_space_constraint(array, pltpu.HBM)


def shape(dims, dtype=F32):
    return jax.ShapeDtypeStruct(dims, dtype)


def units_of(count):
    return (count + (UNIT - 1)) >> 4


def run_copy(table, states_ref, packed_ref, sem, position):
    source = pl.multiple_of(table[0, position] * UNIT, UNIT)
    target = pl.multiple_of(position * UNIT, UNIT)
    return pltpu.make_async_copy(
        states_ref.at[pl.ds(source, UNIT)],
        packed_ref.at[pl.ds(target, UNIT)],
        sem,
    )


def listed(counts, table, start_first):
    me = lax.axis_index("rep")
    owners = counts.shape[0]
    runs = table.shape[1] // owners
    per_block = BLOCK // UNIT

    def put(source, position):
        table[0, position] = source

        @pl.when(position < per_block)
        def _():
            start_first(position)

    def owner(o, position):
        count = counts[o, me]
        table[1, o] = count

        def unit(u, position):
            put(o * runs + u, position)
            return position + 1

        return lax.fori_loop(0, units_of(count), unit, position)

    units = lax.fori_loop(0, owners, owner, jnp.int32(0))
    blocks = (units + (per_block - 1)) >> 4
    lax.fori_loop(units, blocks * per_block, lambda p, c: (put(0, p), c)[1], 0)
    table[1, owners] = blocks


def gathered_block(states_ref, packed_ref, sem):
    return pltpu.make_async_copy(states_ref.at[pl.ds(0, BLOCK)], packed_ref.at[pl.ds(0, BLOCK)], sem)


def pack_rows(table, values, packed_refs):
    owners, cap = values[0].shape
    lane = lax.broadcasted_iota(jnp.int32, (1, cap), 1)
    for ref in packed_refs:
        ref[...] = jnp.zeros_like(ref)
    start = jnp.int32(0)
    for o in range(owners):
        count = table[1, o]
        row, shift = start >> 7, start & 127
        for value, ref in zip(values, packed_refs):
            kept = jnp.where(lane < count, value[o : o + 1, :], 0.0)
            turned = pltpu.roll(kept, shift, 1)
            ref[pl.ds(row, 1), :] += jnp.where(lane >= shift, turned, 0.0)
            ref[pl.ds(row + 1, 1), :] += jnp.where(lane < shift, turned, 0.0)
        start = start + units_of(count) * UNIT


def next_kernel(
    buffer_ref, w_in_ref, w_out_ref, fetch_ref, counts_ref, states_ref,
    picked_ref, w_ref, first_ref, table,
    rows_ref, w_second, fetch, total, counts, sems, small_sems,
):
    steps = sems.shape[1]
    depth = w_in_ref.shape[0] // steps
    counted = pltpu.make_async_copy(counts_ref, counts, small_sems.at[2])
    counted.start()
    copies = []
    for i in range(steps):
        part = pl.ds(i * depth, depth)
        pair = (
            pltpu.make_async_copy(w_in_ref.at[part], w_ref.at[part], sems.at[0, i]),
            pltpu.make_async_copy(buffer_ref.at[:, part], rows_ref.at[:, part], sems.at[1, i]),
        )
        for copy in pair:
            copy.start()
        copies.append(pair)
    second = pltpu.make_async_copy(w_out_ref, w_second, small_sems.at[0])
    wanted = pltpu.make_async_copy(fetch_ref, fetch, small_sems.at[1])
    second.start()
    wanted.start()
    counted.wait()
    listed(
        counts,
        table,
        lambda p: run_copy(table, states_ref, first_ref, small_sems.at[3], p).start(),
    )
    for i in range(steps):
        for copy in copies[i]:
            copy.wait()
        part = pl.ds(i * depth, depth)
        term = jnp.dot(rows_ref[:, part], w_ref[part, :], preferred_element_type=F32)
        total[...] = term if i == 0 else total[...] + term
    preact = total[...]
    hidden = low(preact * jax.nn.sigmoid(preact))
    second.wait()
    wanted.wait()
    logits = jnp.dot(hidden, w_second[...], preferred_element_type=F32)
    best = jax.nn.sigmoid(jnp.max(logits, axis=1, keepdims=True))
    halves = [jnp.broadcast_to(best[i : i + 128], (128, 128)).T[:8] for i in (0, 128)]
    for i in range(0, fetch.shape[0], 8):
        rows = fetch[pl.ds(i, 8), :]
        found = [
            jnp.take_along_axis(half, rows & 127, axis=1, mode="promise_in_bounds")
            for half in halves
        ]
        picked = jnp.where(rows < 128, found[0], found[1])
        for d in range(picked_ref.shape[0]):
            picked_ref[d, pl.ds(i, 8), :] = picked
    gathered_block(states_ref, first_ref, small_sems.at[3]).wait()


def member_kernel(
    table, first_ref, states_ref, w_first, w_second, table_ref, best_ref,
    actions_ref, rewards_ref, terminal_ref, returns_ref,
    targets_ref, packed_ref, d_hidden_ref, grad_ref,
    raw, turned, slope, hidden_now, target_row, scale_row, act_row, sems, start_sems,
):
    me = lax.axis_index("rep")
    owners, cap = rewards_ref.shape
    place_first = pltpu.make_async_copy(
        first_ref, packed_ref.at[pl.ds(0, BLOCK)], start_sems.at[0]
    )
    blocks = table[1, owners]

    def fetch(b):
        @pl.when(b < blocks)
        def _():
            for i in range(BLOCK // UNIT):
                run_copy(
                    table, states_ref, packed_ref, sems.at[b], b * (BLOCK // UNIT) + i
                ).start()

    fetch(jnp.int32(1))

    def arrived(b):
        gathered_block(states_ref, packed_ref, sems.at[b]).wait()

    half = w_first.shape[1] // 2
    halves = (pl.ds(0, half), pl.ds(half, half))

    def begin(b, part):
        rows = pl.ds(pl.multiple_of(b * BLOCK, BLOCK), BLOCK)
        raw[:, part] = jnp.dot(packed_ref[rows, :], w_first[:, part], preferred_element_type=F32)

    def turn(part):
        turned[part, :] = raw[:, part].T

    for part in halves:
        raw[:, part] = jnp.dot(first_ref[...], w_first[:, part], preferred_element_type=F32)
        turn(part)
    counts = table_ref[...]
    counted = jnp.sum(counts).astype(F32)
    requester = lax.broadcasted_iota(jnp.int32, counts.shape, 1)
    mine = jnp.sum(jnp.where(requester == me, counts, 0), axis=1, keepdims=True)
    used = (lax.broadcasted_iota(jnp.int32, (owners, cap), 1) < mine).astype(F32)
    bootstrap = jnp.maximum(jnp.min(best_ref[...], axis=0), returns_ref[...])
    target = rewards_ref[...] + 0.98 * (1.0 - terminal_ref[...].astype(F32)) * bootstrap
    targets_ref[...] = used * target
    scale = used * 2.0 * (jnp.full((owners, cap), 65536.0, F32) / counted)
    pack_rows(
        table, [target, scale, high(actions_ref[...])], [target_row, scale_row, act_row]
    )
    grad_ref[...] = jnp.zeros_like(grad_ref)
    bins = lax.broadcasted_iota(jnp.int32, (grad_ref.shape[1], BLOCK), 0).astype(F32)
    w_out = w_second[...]
    w_out_turned = w_out.T

    def finish(b, following=None):
        at = pl.ds(pl.multiple_of(b * BLOCK, BLOCK), BLOCK)
        goal, scaled, acts = [
            jnp.concatenate([ref[pl.ds(2 * b + i, 1), :] for i in (0, 1)], axis=1)
            for ref in (target_row, scale_row, act_row)
        ]
        preact = turned[...]
        sigmoid_pre = jax.nn.sigmoid(preact)
        hidden_now[...] = low(preact * sigmoid_pre)
        slope[...] = sigmoid_pre * (1.0 + preact * (1.0 - sigmoid_pre))
        if following is not None:
            begin(following, halves[0])
        hidden = hidden_now[...]
        logits = jnp.dot(w_out_turned, hidden, preferred_element_type=F32)
        if following is not None:
            begin(following, halves[1])
            turn(halves[0])
        chosen = bins == acts
        taken = jax.nn.sigmoid(jnp.sum(jnp.where(chosen, logits, 0.0), axis=0, keepdims=True))
        errors = (taken - goal) * taken * (1.0 - taken) * scaled
        d_logits = low(jnp.where(chosen, errors, 0.0))
        grad_ref[...] += lax.dot_general(
            hidden, d_logits, (((1,), (1,)), ((), ())), preferred_element_type=F32
        )
        back = jnp.dot(w_out, d_logits, preferred_element_type=F32)
        d_hidden_ref[:, at] = low(back * slope[...])
        if following is not None:
            turn(halves[1])

    def step(b, carry):
        arrived(b)
        fetch(b + 2)
        finish(b - 1, b)
        return carry

    fetch(jnp.int32(2))
    place_first.start()
    lax.fori_loop(1, blocks, step, 0)
    finish(blocks - 1)
    place_first.wait()


def piece_kernel(steps, parts, with_recv, skip, table, d_hidden_ref, states_ref, grad_ref, *rest):
    recv_ref = rest[0] if with_recv else None
    out_refs, total = (rest[1:-1], rest[-1]) if with_recv else (rest, rest[-1])
    me = lax.axis_index("rep")
    y, x, core = me >> 3, (me >> 1) & 3, me & 1
    blocks = table[1, 16]
    width, depth = d_hidden_ref.shape[0], total.shape[2]
    rows = grad_ref.shape[0] // 16
    first, second = pl.ds(0, width), pl.ds(width, rows)
    ats = [place(y ^ dy, (x + dx) & 3, core ^ dc) for dy, dx, dc in steps]

    for count in range(1, d_hidden_ref.shape[1] // BLOCK + 1):

        @pl.when(blocks == count)
        def _(deep=count * BLOCK):
            def piece(j, carry):
                at = ats[-1]
                for k in range(len(ats) - 1):
                    at = jnp.where(j == k, ats[k], at)
                columns = pl.ds(pl.multiple_of(at * depth, depth), depth)
                term = jnp.dot(
                    d_hidden_ref[:, :deep], states_ref[:deep, columns], preferred_element_type=F32
                )
                if with_recv:
                    term = term + high(recv_ref[j + skip, first, :])
                total[j, first, :] = term.astype(total.dtype)
                return carry

            lax.fori_loop(0, len(ats), piece, 0)

    for j, at in enumerate(ats):
        term = grad_ref[pl.ds(pl.multiple_of(at * rows, rows), rows), :]
        if with_recv:
            term = term + high(recv_ref[j + skip, second, :])
        total[j, second, :] = term.astype(total.dtype)
    for out, (j, start, stop, _) in zip(out_refs, parts or ()):
        out[...] = total[j, pl.ds(start, stop - start), :].astype(out.dtype)


def final_kernel(own_ref, far_ref, first_ref, second_ref):
    width = first_ref.shape[1]
    total = own_ref[...] + high(far_ref[...])
    first_ref[...] = total[:width].T
    second_ref[...] = total[width:]


def update(
    cur_states, buffer, fetch_rows, fetch_counts, actions, rewards, terminal, mc_return, w_in, w_out
):
    w_first, w_second = w_in[0], w_out[0]
    owners, cap = fetch_rows.shape[1:]
    slots, model = cur_states.shape
    width, bins = w_second.shape
    members = lax.axis_size("ens")
    grid = lambda a: a.reshape(owners, cap)

    picked, w_kept, first_block, table = call(
        next_kernel,
        [
            pltpu.VMEM((members, owners, cap), F32),
            pltpu.VMEM(w_first.shape, BF16),
            pltpu.VMEM((BLOCK, model), BF16),
            pltpu.SMEM((8, slots // UNIT), jnp.int32),
        ],
        [HBM] * 6,
        [
            pltpu.VMEM(buffer.shape, BF16),
            pltpu.VMEM(w_second.shape, BF16),
            pltpu.VMEM((owners, cap), jnp.int32),
            pltpu.VMEM((buffer.shape[0], width), F32),
            pltpu.SMEM(fetch_counts.shape, jnp.int32),
            pltpu.SemaphoreType.DMA((2, 8)),
            pltpu.SemaphoreType.DMA((4,)),
        ],
        flops=2 * buffer.shape[0] * model * width,
        bytes_moved=6 << 20,
        out_specs=[VMEM, VMEM, VMEM, SMEM],
    )(
        *[
            in_hbm(a)
            for a in (buffer, w_first, w_second, fetch_rows[0], fetch_counts, cur_states)
        ]
    )
    best = lax.all_to_all(
        picked.reshape(members * owners, 1, cap), ("ens", "rep"), 0, 0, tiled=True
    ).reshape(members, owners, cap)

    targets, packed, d_hidden, grad_second = call(
        member_kernel,
        [
            shape((owners, cap)),
            pltpu.VMEM((slots, model), BF16),
            pltpu.VMEM((width, slots), BF16),
            pltpu.VMEM((width, bins), F32),
        ],
        [SMEM, VMEM, HBM] + [VMEM] * 8,
        [pltpu.VMEM((BLOCK, width), F32)]
        + [pltpu.VMEM((width, BLOCK), F32)] * 2
        + [pltpu.VMEM((width, BLOCK), BF16)]
        + [pltpu.VMEM((owners + 8, cap), F32)] * 3
        + [pltpu.SemaphoreType.DMA((slots // BLOCK,)), pltpu.SemaphoreType.DMA((1,))],
        flops=slots * model * width,
        bytes_moved=14 << 20,
    )(
        table, first_block, in_hbm(cur_states), w_kept, w_second, fetch_counts, best,
        grid(actions), grid(rewards), grid(terminal), grid(mc_return),
    )

    depth = model // 16
    tall = width + width // 16

    def pieces(steps, parts=None, recv=None, skip=0):
        out = (
            shape((len(steps), tall, depth), BF16)
            if parts is None
            else [shape((last - first, depth), dtype) for _, first, last, dtype in parts]
        )
        extra = () if recv is None else (recv,)
        core = 0 if extra else 1
        return call(
            functools.partial(piece_kernel, [(*s, core) for s in steps], parts, len(extra), skip),
            out,
            [SMEM] + [VMEM] * (3 + len(extra)),
            [pltpu.VMEM((len(steps), tall, depth), F32)] if extra else [],
            flops=len(steps) * slots * width * depth,
            bytes_moved=len(steps) << 18,
        )(table, d_hidden, packed, grad_second, *extra)

    other = [(1, 1), (1, 3)]
    middle = [(1, 2), (0, 1), (0, 3)]
    last = [(0, 2), (1, 0), (0, 0)]
    whole = lambda *dtypes: [(j, 0, tall, dtype) for j, dtype in enumerate(dtypes)]

    away_other = sent(pieces(other), CORE)
    away_middle = sent(pieces(middle), CORE)
    right_other, left_other = pieces(other, whole(BF16, BF16), away_other)
    from_left_other = sent(right_other, RIGHT)
    from_right_other = sent(left_other, LEFT)
    (far_other,) = pieces(middle[:1], whole(BF16), away_middle)
    across_far = sent(far_other, ACROSS)
    away_last = sent(pieces(last), CORE)
    right_same, left_same = pieces(middle[1:], whole(BF16, BF16), away_middle, 1)
    from_left_same = sent(right_same, RIGHT)
    from_right_same = sent(left_same, LEFT)
    far_same, own_other, own_same = pieces(last, whole(F32, F32, F32), away_last)
    far_same, own_other, own_same = after(far_same, own_other, own_same)
    from_far = sent(low(far_same + high(across_far)), FAR)
    own_other = own_other + high(from_left_other) + high(from_right_other)
    over = sent(low(own_other), ACROSS)
    own_same = own_same + high(from_left_same) + high(from_right_same) + high(over)
    own_same, from_far = after(own_same, from_far)
    first, second = call(
        final_kernel, [shape((depth, width)), shape((width // 16, bins))], [VMEM] * 2
    )(own_same, from_far)
    return (targets.reshape(-1), first[None], second[None])


def solution(mesh):
    placed = (
        P("rep", None),
        P("rep", None),
        P("rep", None, None),
        P(),
        P("rep"),
        P("rep"),
        P("rep"),
        P("rep"),
        P("ens", None, None),
        P("ens", None, None),
    )
    return jax.shard_map(
        update,
        mesh=mesh,
        in_specs=placed,
        out_specs=(P("rep"), P("ens", "rep", None), P("ens", "rep", None)),
        check_vma=False,
    )
```

```python
import functools

import jax
import jax.numpy as jnp
from jax import lax
from jax.experimental import pallas as pl
from jax.experimental.pallas import tpu as pltpu
from jax.sharding import PartitionSpec as P


UNIT = 16
BLOCK = 256
F32, BF16 = jnp.float32, jnp.bfloat16
VMEM = pl.BlockSpec(memory_space=pltpu.VMEM)
SMEM = pl.BlockSpec(memory_space=pltpu.SMEM)
HBM = pl.BlockSpec(memory_space=pltpu.HBM)


def place(y, x, core):
    return y * 8 + x * 2 + core


def moves(fn):
    return [
        (place(y, x, c), place(*fn(y, x, c)))
        for y in range(2)
        for x in range(4)
        for c in range(2)
    ]


CORE = moves(lambda y, x, c: (y, x, 1 - c))
RIGHT = moves(lambda y, x, c: (y, (x + 1) % 4, c))
LEFT = moves(lambda y, x, c: (y, (x + 3) % 4, c))
FAR = moves(lambda y, x, c: (y, (x + 2) % 4, c))
ACROSS = moves(lambda y, x, c: (1 - y, x, c))


def sent(value, pairs):
    return lax.ppermute(value, "rep", pairs)


def low(value):
    return value.astype(BF16)


def high(value):
    return value.astype(F32)


def after(value, *others):
    return lax.optimization_barrier((value, *others))


def call(
    kernel, out_shape, in_specs, scratch=(), out_specs=None, limit=16, flops=0,
    bytes_moved=1 << 20,
):
    single = not isinstance(out_shape, (list, tuple))
    if out_specs is None:
        out_specs = VMEM if single else [VMEM] * len(out_shape)
    return pl.pallas_call(
        kernel,
        out_shape=out_shape,
        in_specs=in_specs,
        out_specs=out_specs,
        scratch_shapes=list(scratch),
        compiler_params=pltpu.CompilerParams(vmem_limit_bytes=limit << 20),
        cost_estimate=pl.CostEstimate(
            flops=flops, bytes_accessed=bytes_moved, transcendentals=0
        ),
    )


def in_hbm(array):
    return pltpu.with_memory_space_constraint(array, pltpu.HBM)


def shape(dims, dtype=F32):
    return jax.ShapeDtypeStruct(dims, dtype)


def units_of(count):
    return (count + (UNIT - 1)) >> 4


def run_copy(table, states_ref, packed_ref, sem, position):
    source = pl.multiple_of(table[0, position] * UNIT, UNIT)
    target = pl.multiple_of(position * UNIT, UNIT)
    return pltpu.make_async_copy(
        states_ref.at[pl.ds(source, UNIT)],
        packed_ref.at[pl.ds(target, UNIT)],
        sem,
    )


def listed(counts, table):
    me = lax.axis_index("rep")
    owners = counts.shape[0]
    runs = table.shape[1] // owners
    per_block = BLOCK // UNIT

    def put(source, position):
        table[0, position] = source

    def owner(o, position):
        count = counts[o, me]
        table[1, o] = count

        def unit(u, position):
            put(o * runs + u, position)
            return position + 1

        return lax.fori_loop(0, units_of(count), unit, position)

    units = lax.fori_loop(0, owners, owner, jnp.int32(0))
    blocks = (units + (per_block - 1)) >> 4
    lax.fori_loop(units, blocks * per_block, lambda p, c: (put(0, p), c)[1], 0)
    table[1, owners] = blocks


def gathered_block(states_ref, packed_ref, sem):
    return pltpu.make_async_copy(states_ref.at[pl.ds(0, BLOCK)], packed_ref.at[pl.ds(0, BLOCK)], sem)


def pack_rows(table, values, packed_refs):
    owners, cap = values[0].shape
    lane = lax.broadcasted_iota(jnp.int32, (1, cap), 1)
    for ref in packed_refs:
        ref[...] = jnp.zeros_like(ref)
    start = jnp.int32(0)
    for o in range(owners):
        count = table[1, o]
        row, shift = start >> 7, start & 127
        for value, ref in zip(values, packed_refs):
            kept = jnp.where(lane < count, value[o : o + 1, :], 0.0)
            turned = pltpu.roll(kept, shift, 1)
            ref[pl.ds(row, 1), :] += jnp.where(lane >= shift, turned, 0.0)
            ref[pl.ds(row + 1, 1), :] += jnp.where(lane < shift, turned, 0.0)
        start = start + units_of(count) * UNIT


def next_kernel(
    buffer_ref, w_in_ref, w_out_ref, fetch_ref, counts_ref, states_ref,
    picked_ref, w_ref, first_ref, table,
    rows_ref, w_second, fetch, total, counts, sems, small_sems,
):
    steps = sems.shape[1]
    depth = w_in_ref.shape[0] // steps
    counted = pltpu.make_async_copy(counts_ref, counts, small_sems.at[2])
    counted.start()
    copies = []
    for i in range(steps):
        part = pl.ds(i * depth, depth)
        pair = (
            pltpu.make_async_copy(w_in_ref.at[part], w_ref.at[part], sems.at[0, i]),
            pltpu.make_async_copy(buffer_ref.at[:, part], rows_ref.at[:, part], sems.at[1, i]),
        )
        for copy in pair:
            copy.start()
        copies.append(pair)
    second = pltpu.make_async_copy(w_out_ref, w_second, small_sems.at[0])
    wanted = pltpu.make_async_copy(fetch_ref, fetch, small_sems.at[1])
    second.start()
    wanted.start()
    counted.wait()
    listed(counts, table)
    for i in range(steps):
        for copy in copies[i]:
            copy.wait()
        if i == steps // 2:
            for p in range(BLOCK // UNIT):
                run_copy(table, states_ref, first_ref, small_sems.at[3], p).start()
        part = pl.ds(i * depth, depth)
        term = jnp.dot(rows_ref[:, part], w_ref[part, :], preferred_element_type=F32)
        total[...] = term if i == 0 else total[...] + term
    preact = total[...]
    hidden = low(preact * jax.nn.sigmoid(preact))
    second.wait()
    wanted.wait()
    logits = jnp.dot(hidden, w_second[...], preferred_element_type=F32)
    best = jax.nn.sigmoid(jnp.max(logits, axis=1, keepdims=True))
    halves = [jnp.broadcast_to(best[i : i + 128], (128, 128)).T[:8] for i in (0, 128)]
    for i in range(0, fetch.shape[0], 8):
        rows = fetch[pl.ds(i, 8), :]
        found = [
            jnp.take_along_axis(half, rows & 127, axis=1, mode="promise_in_bounds")
            for half in halves
        ]
        picked = jnp.where(rows < 128, found[0], found[1])
        for d in range(picked_ref.shape[0]):
            picked_ref[d, pl.ds(i, 8), :] = picked
    gathered_block(states_ref, first_ref, small_sems.at[3]).wait()


def member_kernel(
    table, first_ref, states_ref, w_first, w_second, table_ref, best_ref,
    actions_ref, rewards_ref, terminal_ref, returns_ref,
    targets_ref, packed_ref, d_hidden_ref, grad_ref,
    raw, turned, slope, hidden_now, target_row, scale_row, act_row, sems, start_sems,
):
    me = lax.axis_index("rep")
    owners, cap = rewards_ref.shape
    place_first = pltpu.make_async_copy(
        first_ref, packed_ref.at[pl.ds(0, BLOCK)], start_sems.at[0]
    )
    blocks = table[1, owners]

    def fetch(b):
        @pl.when(b < blocks)
        def _():
            for i in range(BLOCK // UNIT):
                run_copy(
                    table, states_ref, packed_ref, sems.at[b], b * (BLOCK // UNIT) + i
                ).start()

    fetch(jnp.int32(1))

    def arrived(b):
        gathered_block(states_ref, packed_ref, sems.at[b]).wait()

    half = w_first.shape[1] // 2
    halves = (pl.ds(0, half), pl.ds(half, half))

    def begin(b, part):
        rows = pl.ds(pl.multiple_of(b * BLOCK, BLOCK), BLOCK)
        raw[:, part] = jnp.dot(packed_ref[rows, :], w_first[:, part], preferred_element_type=F32)

    def turn(part):
        turned[part, :] = raw[:, part].T

    for part in halves:
        raw[:, part] = jnp.dot(first_ref[...], w_first[:, part], preferred_element_type=F32)
        turn(part)
    counts = table_ref[...]
    counted = jnp.sum(counts).astype(F32)
    requester = lax.broadcasted_iota(jnp.int32, counts.shape, 1)
    mine = jnp.sum(jnp.where(requester == me, counts, 0), axis=1, keepdims=True)
    used = (lax.broadcasted_iota(jnp.int32, (owners, cap), 1) < mine).astype(F32)
    bootstrap = jnp.maximum(jnp.min(best_ref[...], axis=0), returns_ref[...])
    target = rewards_ref[...] + 0.98 * (1.0 - terminal_ref[...].astype(F32)) * bootstrap
    targets_ref[...] = used * target
    scale = used * 2.0 * (jnp.full((owners, cap), 65536.0, F32) / counted)
    pack_rows(
        table, [target, scale, high(actions_ref[...])], [target_row, scale_row, act_row]
    )
    grad_ref[...] = jnp.zeros_like(grad_ref)
    bins = lax.broadcasted_iota(jnp.int32, (grad_ref.shape[1], BLOCK), 0).astype(F32)
    w_out = w_second[...]
    w_out_turned = w_out.T

    def finish(b, following=None):
        at = pl.ds(pl.multiple_of(b * BLOCK, BLOCK), BLOCK)
        goal, scaled, acts = [
            jnp.concatenate([ref[pl.ds(2 * b + i, 1), :] for i in (0, 1)], axis=1)
            for ref in (target_row, scale_row, act_row)
        ]
        preact = turned[...]
        sigmoid_pre = jax.nn.sigmoid(preact)
        hidden_now[...] = low(preact * sigmoid_pre)
        slope[...] = sigmoid_pre * (1.0 + preact * (1.0 - sigmoid_pre))
        if following is not None:
            begin(following, halves[0])
        hidden = hidden_now[...]
        logits = jnp.dot(w_out_turned, hidden, preferred_element_type=F32)
        if following is not None:
            begin(following, halves[1])
            turn(halves[0])
        chosen = bins == acts
        taken = jax.nn.sigmoid(jnp.sum(jnp.where(chosen, logits, 0.0), axis=0, keepdims=True))
        errors = (taken - goal) * taken * (1.0 - taken) * scaled
        d_logits = low(jnp.where(chosen, errors, 0.0))
        grad_ref[...] += lax.dot_general(
            hidden, d_logits, (((1,), (1,)), ((), ())), preferred_element_type=F32
        )
        back = jnp.dot(w_out, d_logits, preferred_element_type=F32)
        d_hidden_ref[:, at] = low(back * slope[...])
        if following is not None:
            turn(halves[1])

    def step(b, carry):
        arrived(b)
        fetch(b + 2)
        finish(b - 1, b)
        return carry

    fetch(jnp.int32(2))
    place_first.start()
    lax.fori_loop(1, blocks, step, 0)
    finish(blocks - 1)
    place_first.wait()


def piece_kernel(steps, parts, with_recv, skip, table, d_hidden_ref, states_ref, grad_ref, *rest):
    recv_ref = rest[0] if with_recv else None
    out_refs, total = (rest[1:-1], rest[-1]) if with_recv else (rest, rest[-1])
    me = lax.axis_index("rep")
    y, x, core = me >> 3, (me >> 1) & 3, me & 1
    blocks = table[1, 16]
    width, depth = d_hidden_ref.shape[0], total.shape[2]
    rows = grad_ref.shape[0] // 16
    first, second = pl.ds(0, width), pl.ds(width, rows)
    ats = [place(y ^ dy, (x + dx) & 3, core ^ dc) for dy, dx, dc in steps]

    for count in range(1, d_hidden_ref.shape[1] // BLOCK + 1):

        @pl.when(blocks == count)
        def _(deep=count * BLOCK):
            def piece(j, carry):
                at = ats[-1]
                for k in range(len(ats) - 1):
                    at = jnp.where(j == k, ats[k], at)
                columns = pl.ds(pl.multiple_of(at * depth, depth), depth)
                term = jnp.dot(
                    d_hidden_ref[:, :deep], states_ref[:deep, columns], preferred_element_type=F32
                )
                if with_recv:
                    term = term + high(recv_ref[j + skip, first, :])
                total[j, first, :] = term.astype(total.dtype)
                return carry

            lax.fori_loop(0, len(ats), piece, 0)

    for j, at in enumerate(ats):
        term = grad_ref[pl.ds(pl.multiple_of(at * rows, rows), rows), :]
        if with_recv:
            term = term + high(recv_ref[j + skip, second, :])
        total[j, second, :] = term.astype(total.dtype)
    for out, (j, start, stop, _) in zip(out_refs, parts or ()):
        out[...] = total[j, pl.ds(start, stop - start), :].astype(out.dtype)


def final_kernel(own_ref, far_ref, first_ref, second_ref):
    width = first_ref.shape[1]
    total = own_ref[...] + high(far_ref[...])
    first_ref[...] = total[:width].T
    second_ref[...] = total[width:]


def update(
    cur_states, buffer, fetch_rows, fetch_counts, actions, rewards, terminal, mc_return, w_in, w_out
):
    w_first, w_second = w_in[0], w_out[0]
    owners, cap = fetch_rows.shape[1:]
    slots, model = cur_states.shape
    width, bins = w_second.shape
    members = lax.axis_size("ens")
    grid = lambda a: a.reshape(owners, cap)

    picked, w_kept, first_block, table = call(
        next_kernel,
        [
            pltpu.VMEM((members, owners, cap), F32),
            pltpu.VMEM(w_first.shape, BF16),
            pltpu.VMEM((BLOCK, model), BF16),
            pltpu.SMEM((8, slots // UNIT), jnp.int32),
        ],
        [HBM] * 6,
        [
            pltpu.VMEM(buffer.shape, BF16),
            pltpu.VMEM(w_second.shape, BF16),
            pltpu.VMEM((owners, cap), jnp.int32),
            pltpu.VMEM((buffer.shape[0], width), F32),
            pltpu.SMEM(fetch_counts.shape, jnp.int32),
            pltpu.SemaphoreType.DMA((2, 8)),
            pltpu.SemaphoreType.DMA((4,)),
        ],
        flops=2 * buffer.shape[0] * model * width,
        bytes_moved=6 << 20,
        out_specs=[VMEM, VMEM, VMEM, SMEM],
    )(
        *[
            in_hbm(a)
            for a in (buffer, w_first, w_second, fetch_rows[0], fetch_counts, cur_states)
        ]
    )
    best = lax.all_to_all(
        picked.reshape(members * owners, 1, cap), ("ens", "rep"), 0, 0, tiled=True
    ).reshape(members, owners, cap)

    targets, packed, d_hidden, grad_second = call(
        member_kernel,
        [
            shape((owners, cap)),
            pltpu.VMEM((slots, model), BF16),
            pltpu.VMEM((width, slots), BF16),
            pltpu.VMEM((width, bins), F32),
        ],
        [SMEM, VMEM, HBM] + [VMEM] * 8,
        [pltpu.VMEM((BLOCK, width), F32)]
        + [pltpu.VMEM((width, BLOCK), F32)] * 2
        + [pltpu.VMEM((width, BLOCK), BF16)]
        + [pltpu.VMEM((owners + 8, cap), F32)] * 3
        + [pltpu.SemaphoreType.DMA((slots // BLOCK,)), pltpu.SemaphoreType.DMA((1,))],
        flops=slots * model * width,
        bytes_moved=14 << 20,
    )(
        table, first_block, in_hbm(cur_states), w_kept, w_second, fetch_counts, best,
        grid(actions), grid(rewards), grid(terminal), grid(mc_return),
    )

    depth = model // 16
    tall = width + width // 16

    def pieces(steps, parts=None, recv=None, skip=0):
        out = (
            shape((len(steps), tall, depth), BF16)
            if parts is None
            else [shape((last - first, depth), dtype) for _, first, last, dtype in parts]
        )
        extra = () if recv is None else (recv,)
        core = 0 if extra else 1
        return call(
            functools.partial(piece_kernel, [(*s, core) for s in steps], parts, len(extra), skip),
            out,
            [SMEM] + [VMEM] * (3 + len(extra)),
            [pltpu.VMEM((len(steps), tall, depth), F32)] if extra else [],
            flops=len(steps) * slots * width * depth,
            bytes_moved=len(steps) << 18,
        )(table, d_hidden, packed, grad_second, *extra)

    other = [(1, 1), (1, 3)]
    middle = [(1, 2), (0, 1), (0, 3)]
    last = [(0, 2), (1, 0), (0, 0)]
    whole = lambda *dtypes: [(j, 0, tall, dtype) for j, dtype in enumerate(dtypes)]

    away_other = sent(pieces(other), CORE)
    away_middle = sent(pieces(middle), CORE)
    right_other, left_other = pieces(other, whole(BF16, BF16), away_other)
    from_left_other = sent(right_other, RIGHT)
    from_right_other = sent(left_other, LEFT)
    (far_other,) = pieces(middle[:1], whole(BF16), away_middle)
    across_far = sent(far_other, ACROSS)
    away_last = sent(pieces(last), CORE)
    right_same, left_same = pieces(middle[1:], whole(BF16, BF16), away_middle, 1)
    from_left_same = sent(right_same, RIGHT)
    from_right_same = sent(left_same, LEFT)
    far_same, own_other, own_same = pieces(last, whole(F32, F32, F32), away_last)
    far_same, own_other, own_same = after(far_same, own_other, own_same)
    from_far = sent(low(far_same + high(across_far)), FAR)
    own_other = own_other + high(from_left_other) + high(from_right_other)
    over = sent(low(own_other), ACROSS)
    own_same = own_same + high(from_left_same) + high(from_right_same) + high(over)
    own_same, from_far = after(own_same, from_far)
    first, second = call(
        final_kernel, [shape((depth, width)), shape((width // 16, bins))], [VMEM] * 2
    )(own_same, from_far)
    return (targets.reshape(-1), first[None], second[None])


def solution(mesh):
    placed = (
        P("rep", None),
        P("rep", None),
        P("rep", None, None),
        P(),
        P("rep"),
        P("rep"),
        P("rep"),
        P("rep"),
        P("ens", None, None),
        P("ens", None, None),
    )
    return jax.shard_map(
        update,
        mesh=mesh,
        in_specs=placed,
        out_specs=(P("rep"), P("ens", "rep", None), P("ens", "rep", None)),
        check_vma=False,
    )
```
